512 devices in a mesh: gx: 16 (over y, z_hi), gy: 32 (over x, z_lo, core).
Axes of the slice: x: 4, y: 8, z: 8 (z_hi: 2, z_lo: 4; z = z_hi * 4 + z_lo), core: 2. Of those that a mesh axis runs over, the one named last changes fastest.
Arguments:
- e_field: float32 [3, 8, 2048, 2048], P(None, None, 'gy', 'gx'), may hold values from -7 to 7
- h_field: float32 [3, 8, 2048, 2048], P(None, None, 'gy', 'gx'), may hold values from -7 to 7
- material: int32 [8, 2048, 2048], P(None, 'gy', 'gx'), may hold values from 0 to 7
- permittivity: float32 [8], replicated, may hold values from 1 to 12
- conductivity: float32 [8], replicated, may hold values from 0.01 to 2
- wire_layers: int32 [8], replicated, may hold values from 0 to 1, as said below
Outputs:
- e_next: float32 [3, 8, 2048, 2048], P(None, None, 'gy', 'gx')
- h_next: float32 [3, 8, 2048, 2048], P(None, None, 'gy', 'gx')
The draws below stay inside these ranges and needn't reach their ends.
Inputs may be any that keep to these rules, and one draw needn't show every extreme that they name: `wire_layers`: exactly 4 entries are 1.
All inputs are finite; a program needn't handle non-finite values.
Results may differ from the reference program's by a relative error of at most 0.0004.
The reference program's roundings to bfloat16 on the way count: a program that leaves them out, or rounds other values in their place, can miss the bound.
Values may be sent and summed in bfloat16 or wider, within the bound.
A program may use at most 128 MiB of HBM per device.

```python
import math
import jax
import jax.numpy as jnp
from jax import lax

NZ = 8
MATS = 8
NX = 2048
NY = 2048


def draw_wire_layers(key, part):
    shuffled = jax.random.permutation(key, NZ)
    return jnp.where(shuffled < NZ // 2, 1, 0).astype(jnp.int32)


def line_field(key):
    noise_key, freq_key, phase_key = jax.random.split(key, 3)
    shape = (3, NZ, NY, NX)
    rows = jnp.arange(NY, dtype=jnp.int32)[None, None, :, None]
    freq = jax.random.randint(freq_key, (3, NZ, 1, 1), NY // 4 - 2, NY // 4 + 3)
    phase = jax.random.uniform(phase_key, (3, NZ, 1, 1), jnp.float32, -math.pi, math.pi)
    turned = jnp.mod(freq * rows, NY).astype(jnp.float32)
    tone = jnp.cos(2.0 * math.pi * turned / NY + phase)
    noise = jnp.clip(jax.random.normal(noise_key, shape, jnp.float32), -6.0, 6.0)
    return (noise + tone).astype(jnp.float32)


def draw_e_field(key, part):
    return line_field(jax.random.fold_in(key, 11))


def draw_h_field(key, part):
    return line_field(jax.random.fold_in(key, 23))


def place_ends(array, rng, low, high):
    extent = array.shape
    place = [jax.random.randint(jax.random.fold_in(rng, axis), (), 0, extent[axis]) for axis in range(len(extent))]
    array = array.at[tuple(place)].set(low)
    longest = extent.index(max(extent))
    place[longest] = (place[longest] + 1) % extent[longest]
    return array.at[tuple(place)].set(high)


def setup_inputs(seed: int = 0) -> dict:
    key_list = jax.random.split(jax.random.key(seed), 7)
    e_field = draw_e_field(jax.random.fold_in(key_list[6], 71), 0)
    h_field = draw_h_field(jax.random.fold_in(key_list[6], 71), 0)
    material = place_ends(jax.random.randint(key_list[2], (NZ, NY, NX), 0, MATS), jax.random.fold_in(key_list[2], 1), 0, MATS - 1).astype(jnp.int32)
    permittivity = jnp.clip(jnp.exp(jax.random.uniform(key_list[3], (MATS,), jnp.float32, math.log(1.0), math.log(12.0))), 1.0, 12.0)
    conductivity = jnp.clip(jnp.exp(jax.random.uniform(key_list[4], (MATS,), jnp.float32, math.log(0.01), math.log(2.0))), 0.01, 2.0)
    wire_layers = draw_wire_layers(jax.random.fold_in(key_list[6], 71), 0)
    return dict(e_field=e_field, h_field=h_field, material=material, permittivity=permittivity, conductivity=conductivity, wire_layers=wire_layers)


TIME_STEP = 0.9


def filter_rows(first_idx, n_rows, n_cols):
    row_pos = first_idx + jnp.arange(n_rows, dtype=jnp.int32)
    col_pos = jnp.arange(n_cols, dtype=jnp.int32)
    delta = row_pos[:, None] - col_pos[None, :]
    modes = 2 * (n_cols // 4) + 1
    turned = jnp.mod(modes * delta, 2 * n_cols)
    safe_delta = jnp.where(delta == 0, 1, delta)
    upper = jnp.sin(math.pi * turned.astype(jnp.float32) / n_cols)
    lower = n_cols * jnp.sin(math.pi * safe_delta.astype(jnp.float32) / n_cols)
    band = jnp.where(delta == 0, modes / n_cols, upper / lower)
    return (0.7 * band + jnp.where(delta == 0, 0.3, 0.0)).astype(jnp.bfloat16)


def ahead_of(comp, along):
    n_len = comp.shape[along]
    rest = lax.slice_in_dim(comp, 1, n_len, axis=along)
    zeros = jnp.zeros_like(lax.slice_in_dim(comp, 0, 1, axis=along))
    return jnp.concatenate([rest, zeros], axis=along) - comp


def behind_of(comp, along):
    n_len = comp.shape[along]
    rest = lax.slice_in_dim(comp, 0, n_len - 1, axis=along)
    zeros = jnp.zeros_like(lax.slice_in_dim(comp, 0, 1, axis=along))
    return comp - jnp.concatenate([zeros, rest], axis=along)


def curl_of_e(e_field):
    e_x, e_y, e_z = e_field[0], e_field[1], e_field[2]
    curl_x = ahead_of(e_z, 1) - ahead_of(e_y, 0)
    curl_y = ahead_of(e_x, 0) - (jnp.roll(e_z, -1, 2) - e_z)
    curl_z = (jnp.roll(e_y, -1, 2) - e_y) - ahead_of(e_x, 1)
    return jnp.stack([curl_x, curl_y, curl_z])


def curl_of_h(h_field):
    h_x, h_y, h_z = h_field[0], h_field[1], h_field[2]
    curl_x = behind_of(h_z, 1) - behind_of(h_y, 0)
    curl_y = behind_of(h_x, 0) - (h_z - jnp.roll(h_z, 1, 2))
    curl_z = (h_y - jnp.roll(h_y, 1, 2)) - behind_of(h_x, 1)
    return jnp.stack([curl_x, curl_y, curl_z])


def smooth(field_in, f_matrix, wire_layers):
    rounded = field_in.astype(jnp.bfloat16)
    filtered = jnp.einsum("mn,cznx->czmx", f_matrix.astype(jnp.float32), rounded.astype(jnp.float32))
    return jnp.where(wire_layers[None, :, None, None] == 1, filtered, field_in)


def reference(e_field, h_field, material, permittivity, conductivity, wire_layers):
    n_lines = e_field.shape[2]
    f_matrix = filter_rows(0, n_lines, n_lines)
    h_half = h_field - TIME_STEP * curl_of_e(e_field)
    h_next = smooth(h_half, f_matrix, wire_layers)
    eps = permittivity[material]
    sig = conductivity[material]
    ratio = sig * TIME_STEP / (2.0 * eps)
    decay = (1.0 - ratio) / (1.0 + ratio)
    gain = (TIME_STEP / eps) / (1.0 + ratio)
    e_half = decay[None] * e_field + gain[None] * curl_of_h(h_next)
    e_next = smooth(e_half, f_matrix, wire_layers)
    return e_next, h_next
```

```python
import math

import jax
import jax.numpy as jnp
from jax import lax
from jax.sharding import PartitionSpec as P

TIME_STEP = 0.9


def shifted(value, axis, steps):
    count = lax.axis_size(axis)
    pairs = [(source, (source + steps) % count) for source in range(count)]
    return lax.ppermute(value, axis, pairs)


def passed_along(shard, axis, by):
    devices = lax.axis_size(axis)
    pairs = [(i, i + by) for i in range(devices) if 0 <= i + by < devices]
    return lax.ppermute(shard, axis, pairs)


def filter_rows(first_idx, n_rows, n_cols):
    row_pos = first_idx + jnp.arange(n_rows, dtype=jnp.int32)
    col_pos = jnp.arange(n_cols, dtype=jnp.int32)
    delta = row_pos[:, None] - col_pos[None, :]
    modes = 2 * (n_cols // 4) + 1
    turned = jnp.mod(modes * delta, 2 * n_cols)
    safe_delta = jnp.where(delta == 0, 1, delta)
    upper = jnp.sin(math.pi * turned.astype(jnp.float32) / n_cols)
    lower = n_cols * jnp.sin(math.pi * safe_delta.astype(jnp.float32) / n_cols)
    band = jnp.where(delta == 0, modes / n_cols, upper / lower)
    return (0.7 * band + jnp.where(delta == 0, 0.3, 0.0)).astype(jnp.bfloat16)


def face_x(planes, direction):
    return shifted(planes, "gx", direction)


def face_y(planes, direction):
    return passed_along(planes, "gy", direction)


def ahead_z(comp):
    zeros = jnp.zeros_like(comp[:1])
    return jnp.concatenate([comp[1:], zeros], axis=0) - comp


def behind_z(comp):
    zeros = jnp.zeros_like(comp[:1])
    return comp - jnp.concatenate([zeros, comp[:-1]], axis=0)


def ahead_x(comp, edge_col):
    return jnp.concatenate([comp[:, :, 1:], edge_col[:, :, None]], axis=2) - comp


def behind_x(comp, edge_col):
    return comp - jnp.concatenate([edge_col[:, :, None], comp[:, :, :-1]], axis=2)


def ahead_y(comp, edge_row):
    return jnp.concatenate([comp[:, 1:, :], edge_row[:, None, :]], axis=1) - comp


def behind_y(comp, edge_row):
    return comp - jnp.concatenate([edge_row[:, None, :], comp[:, :-1, :]], axis=1)


def curl_of_e(e_field):
    next_x = face_x(e_field[1:3, :, :, 0], -1)
    next_y = face_y(jnp.stack([e_field[0, :, 0, :], e_field[2, :, 0, :]]), -1)
    e_x, e_y, e_z = (e_field[0], e_field[1], e_field[2])
    curl_x = ahead_y(e_z, next_y[1]) - ahead_z(e_y)
    curl_y = ahead_z(e_x) - ahead_x(e_z, next_x[1])
    curl_z = ahead_x(e_y, next_x[0]) - ahead_y(e_x, next_y[0])
    return jnp.stack([curl_x, curl_y, curl_z])


def curl_of_h(h_field):
    last_col = h_field.shape[3] - 1
    last_row = h_field.shape[2] - 1
    prev_x = face_x(h_field[1:3, :, :, last_col], 1)
    prev_y = face_y(jnp.stack([h_field[0, :, last_row, :], h_field[2, :, last_row, :]]), 1)
    h_x, h_y, h_z = (h_field[0], h_field[1], h_field[2])
    curl_x = behind_y(h_z, prev_y[1]) - behind_z(h_y)
    curl_y = behind_z(h_x) - behind_x(h_z, prev_x[1])
    curl_z = behind_x(h_y, prev_x[0]) - behind_y(h_x, prev_y[0])
    return jnp.stack([curl_x, curl_y, curl_z])


def smooth(field_in, wire_layers):
    block_rows = field_in.shape[2]
    n_layers = field_in.shape[1]
    n_wires = n_layers // 2
    n_lines = block_rows * lax.axis_size("gy")
    rank = jnp.cumsum(wire_layers) - 1
    slots = jnp.arange(n_wires, dtype=jnp.int32)
    picked = (wire_layers[None] == 1) & (rank[None] == slots[:, None])
    layer_of = jnp.sum(jnp.where(picked, jnp.arange(n_layers, dtype=jnp.int32)[None], 0), axis=1)
    wires = jnp.concatenate(
        [lax.dynamic_slice_in_dim(field_in, layer_of[k], 1, axis=1) for k in range(n_wires)], axis=1
    )
    rounded = wires.astype(jnp.bfloat16)
    f_rows = filter_rows(lax.axis_index("gy") * block_rows, block_rows, n_lines)
    filtered = jnp.einsum(
        "mn,cznx->czmx",
        f_rows,
        lax.all_gather(rounded, "gy", axis=2, tiled=True),
        preferred_element_type=jnp.float32,
    )
    out = field_in
    for k in range(n_wires):
        out = lax.dynamic_update_slice_in_dim(out, filtered[:, k : k + 1], layer_of[k], axis=1)
    return out


def body(e_field, h_field, material, permittivity, conductivity, wire_layers):
    h_half = h_field - TIME_STEP * curl_of_e(e_field)
    h_next = smooth(h_half, wire_layers)
    ratio_tab = conductivity * TIME_STEP / (2.0 * permittivity)
    decay_tab = (1.0 - ratio_tab) / (1.0 + ratio_tab)
    gain_tab = TIME_STEP / permittivity / (1.0 + ratio_tab)
    labels = jnp.arange(permittivity.shape[0], dtype=jnp.int32)
    onehot = (material[None] == labels[:, None, None, None]).astype(jnp.float32)
    decay = jnp.sum(onehot * decay_tab[:, None, None, None], axis=0)
    gain = jnp.sum(onehot * gain_tab[:, None, None, None], axis=0)
    e_half = decay[None] * e_field + gain[None] * curl_of_h(h_next)
    e_next = smooth(e_half, wire_layers)
    return (e_next, h_next)


def solution(mesh):
    placed = (
        P(None, None, "gy", "gx"),
        P(None, None, "gy", "gx"),
        P(None, "gy", "gx"),
        P(),
        P(),
        P(),
    )
    return jax.shard_map(
        body,
        mesh=mesh,
        in_specs=placed,
        out_specs=(P(None, None, "gy", "gx"), P(None, None, "gy", "gx")),
        check_vma=False,
    )
```

```python
import functools
import math

import jax
import jax.numpy as jnp
import ml_dtypes
import numpy as np
from jax import lax
from jax.experimental import pallas as pl
from jax.experimental.pallas import tpu as pltpu
from jax.sharding import PartitionSpec as P

TIME_STEP = 0.9
MESH = pl.DeviceIdType.MESH
F32 = jnp.float32
BF16 = jnp.bfloat16
TILE = 256


def filter_strip(n_cols, tile):
    row_pos = np.arange(tile, dtype=np.int64)[:, None]
    col_pos = np.arange(2 * n_cols - tile, dtype=np.int64)[None, :]
    delta = row_pos - col_pos + (n_cols - tile)
    modes = 2 * (n_cols // 4) + 1
    turned = np.mod(modes * delta, 2 * n_cols)
    safe_delta = np.where(delta == 0, 1, delta)
    pi = np.float32(math.pi)
    upper = np.sin(pi * turned.astype(np.float32) / np.float32(n_cols))
    lower = np.float32(n_cols) * np.sin(pi * safe_delta.astype(np.float32) / np.float32(n_cols))
    band = np.where(delta == 0, np.float32(modes / n_cols), upper / lower)
    out = np.float32(0.7) * band + np.where(delta == 0, np.float32(0.3), np.float32(0.0))
    return out.astype(np.float32).astype(ml_dtypes.bfloat16)


def owner_of(plane):
    run = plane // 3
    spot = plane % 3 + 1 - run % 2
    return (run * 4 + spot) * 2 + plane % 2


def kernel(
    n_gx, n_gy, n_wires,
    eps_ref, sig_ref, wire_ref, e_ref, h_ref, mat_ref, strip_hbm,
    e_out, h_out,
    strip, xsend, xrecv, ysend, yrecv, wires, lines, res, filt, decay, gain,
    halo_send, halo_recv, wire_send, line_recv, res_send, ret_recv, strip_sem,
):
    _, nz, rows, cols = e_ref.shape
    n_planes = 3 * n_wires
    n_lines = n_gy * rows
    blocks = n_lines // TILE
    per_block = TILE // rows
    gx = lax.axis_index("gx")
    gy = lax.axis_index("gy")

    barrier = pltpu.get_barrier_semaphore()
    for step in (1, n_gx - 1):
        pl.semaphore_signal(
            barrier, inc=1, device_id={"gx": lax.rem(gx + step, n_gx)}, device_id_type=MESH
        )

    def greet(k, _):
        pl.semaphore_signal(
            barrier, inc=1, device_id={"gy": lax.rem(gy + k, n_gy)}, device_id_type=MESH
        )
        return 0

    lax.fori_loop(1, n_gy, greet, 0)

    strip_copy = pltpu.make_async_copy(strip_hbm, strip, strip_sem)
    strip_copy.start()

    lane = lax.broadcasted_iota(jnp.int32, (rows, cols), 1)
    row = lax.broadcasted_iota(jnp.int32, (rows, cols), 0)

    is_wire = [wire_ref[z] for z in range(nz)]
    rank, layer_of, seen = [], [jnp.int32(0)] * n_wires, jnp.int32(0)
    for z in range(nz):
        rank.append(jnp.minimum(seen, n_wires - 1))
        for k in range(n_wires):
            layer_of[k] = layer_of[k] + jnp.where((is_wire[z] == 1) & (seen == k), z, 0)
        seen = seen + is_wire[z]

    def pack_edges(phase, src, col, edge_row):
        total = jnp.zeros((rows, cols), F32)
        for c in (1, 2):
            for z in range(nz):
                j = (c - 1) * nz + z
                moved = pltpu.roll(src[c, z], (j - col) % cols, 1)
                total = jnp.where(lane == j, moved, total)
        xsend[phase] = total
        for i, c in enumerate((0, 2)):
            for z in range(nz):
                ysend[phase, i * nz + z : i * nz + z + 1, :] = src[c, z, edge_row : edge_row + 1, :]

    def halo_copies(phase, step):
        x_copy = pltpu.make_async_remote_copy(
            src_ref=xsend.at[phase],
            dst_ref=xrecv.at[phase],
            send_sem=halo_send.at[phase, 0],
            recv_sem=halo_recv.at[phase, 0],
            device_id={"gx": lax.rem(gx + step + n_gx, n_gx)},
            device_id_type=MESH,
        )
        y_copy = pltpu.make_async_remote_copy(
            src_ref=ysend.at[phase],
            dst_ref=yrecv.at[phase],
            send_sem=halo_send.at[phase, 1],
            recv_sem=halo_recv.at[phase, 1],
            device_id={"gy": lax.rem(gy + step + n_gy, n_gy)},
            device_id_type=MESH,
        )
        return x_copy, y_copy

    def start_halo(phase, step):
        x_copy, y_copy = halo_copies(phase, step)
        x_copy.start()
        sender = gy > 0 if step < 0 else gy < n_gy - 1

        @pl.when(sender)
        def _():
            y_copy.start()

    def finish_halo(phase, step):
        x_copy, y_copy = halo_copies(phase, step)
        x_copy.wait()
        sender = gy > 0 if step < 0 else gy < n_gy - 1
        receiver = gy < n_gy - 1 if step < 0 else gy > 0

        @pl.when(sender)
        def _():
            y_copy.wait_send()

        @pl.when(receiver)
        def _():
            y_copy.wait_recv()

    def start_wires(phase, src):
        for c in range(3):
            for k in range(n_wires):
                wires[phase, c * n_wires + k] = src[c, layer_of[k]].astype(BF16)

        def send(t, _):
            plane = lax.rem(t + gy, n_planes)
            owner = owner_of(plane)

            @pl.when(owner != gy)
            def _():
                pltpu.make_async_remote_copy(
                    src_ref=wires.at[phase, plane],
                    dst_ref=lines.at[phase, gy],
                    send_sem=wire_send.at[phase, plane],
                    recv_sem=line_recv.at[phase, gy],
                    device_id={"gy": owner},
                    device_id_type=MESH,
                ).start()

            @pl.when(owner == gy)
            def _():
                pltpu.make_async_copy(
                    wires.at[phase, plane], lines.at[phase, gy], line_recv.at[phase, gy]
                ).start()

            return 0

        lax.fori_loop(0, n_planes, send, 0)

    chip = gy // 2
    run = chip // 4
    spot = chip % 4 - 1 + run % 2
    my_plane = run * 3 + jnp.clip(spot, 0, 2)
    i_own = owner_of(my_plane) == gy

    def filter_lines(phase):
        @pl.when(i_own)
        def _():
            def arrive(s, _):
                @pl.when(s != gy)
                def _():
                    pltpu.make_async_remote_copy(
                        src_ref=wires.at[phase, my_plane],
                        dst_ref=lines.at[phase, s],
                        send_sem=wire_send.at[phase, my_plane],
                        recv_sem=line_recv.at[phase, s],
                        device_id={"gy": s},
                        device_id_type=MESH,
                    ).wait_recv()

                @pl.when(s == gy)
                def _():
                    pltpu.make_async_copy(
                        wires.at[phase, my_plane], lines.at[phase, s], line_recv.at[phase, s]
                    ).wait()

                return 0

            lax.fori_loop(0, n_gy, arrive, 0)
            if phase == 0:
                strip_copy.wait()

            def block(t, _):
                at = lax.rem(t + my_plane, blocks)
                start = pl.multiple_of((blocks - 1 - at) * TILE, TILE)
                out = jnp.dot(
                    strip[:, pl.ds(start, n_lines)],
                    lines[phase].reshape(n_lines, cols),
                    preferred_element_type=F32,
                )
                res[phase, pl.ds(at * per_block, per_block)] = out.reshape(per_block, rows, cols)

                def give(i, _):
                    to = at * per_block + i

                    @pl.when(to != gy)
                    def _():
                        pltpu.make_async_remote_copy(
                            src_ref=res.at[phase, to],
                            dst_ref=filt.at[phase, my_plane],
                            send_sem=res_send.at[phase, to],
                            recv_sem=ret_recv.at[phase, my_plane],
                            device_id={"gy": to},
                            device_id_type=MESH,
                        ).start()

                    @pl.when(to == gy)
                    def _():
                        pltpu.make_async_copy(
                            res.at[phase, to], filt.at[phase, my_plane], ret_recv.at[phase, my_plane]
                        ).start()

                    return 0

                lax.fori_loop(0, per_block, give, 0)
                return 0

            lax.fori_loop(0, blocks, block, 0)

    def back(phase):
        def arrive(plane, _):
            owner = owner_of(plane)

            @pl.when(owner != gy)
            def _():
                pltpu.make_async_remote_copy(
                    src_ref=res.at[phase, gy],
                    dst_ref=filt.at[phase, plane],
                    send_sem=res_send.at[phase, gy],
                    recv_sem=ret_recv.at[phase, plane],
                    device_id={"gy": owner},
                    device_id_type=MESH,
                ).wait_recv()

            @pl.when(owner == gy)
            def _():
                pltpu.make_async_copy(
                    res.at[phase, gy], filt.at[phase, plane], ret_recv.at[phase, plane]
                ).wait()

            return 0

        lax.fori_loop(0, n_planes, arrive, 0)

    def drain(phase):
        def wire_gone(plane, _):
            owner = owner_of(plane)

            @pl.when(owner != gy)
            def _():
                pltpu.make_async_remote_copy(
                    src_ref=wires.at[phase, plane],
                    dst_ref=lines.at[phase, gy],
                    send_sem=wire_send.at[phase, plane],
                    recv_sem=line_recv.at[phase, gy],
                    device_id={"gy": owner},
                    device_id_type=MESH,
                ).wait_send()

            return 0

        lax.fori_loop(0, n_planes, wire_gone, 0)

        @pl.when(i_own)
        def _():
            def row_gone(to, _):
                @pl.when(to != gy)
                def _():
                    pltpu.make_async_remote_copy(
                        src_ref=res.at[phase, to],
                        dst_ref=filt.at[phase, my_plane],
                        send_sem=res_send.at[phase, to],
                        recv_sem=ret_recv.at[phase, my_plane],
                        device_id={"gy": to},
                        device_id_type=MESH,
                    ).wait_send()

                return 0

            lax.fori_loop(0, n_gy, row_gone, 0)

    def merge(phase, dst):
        for z in range(nz):
            chosen = jnp.full((rows, cols), is_wire[z], jnp.int32) == 1
            for c in range(3):
                dst[c, z] = jnp.where(chosen, filt[phase, c * n_wires + rank[z]], dst[c, z])

    pack_edges(0, e_ref, 0, 0)

    @pl.when(gy == n_gy - 1)
    def _():
        yrecv[0] = jnp.zeros((2 * nz, cols), F32)

    @pl.when(gy == 0)
    def _():
        yrecv[1] = jnp.zeros((2 * nz, cols), F32)

    pl.semaphore_wait(barrier, n_gy + 1)
    start_halo(0, -1)

    tables = []
    for m in range(eps_ref.shape[0]):
        eps = jnp.full((8, cols), eps_ref[m], F32)
        ratio = jnp.full((8, cols), sig_ref[m], F32) * TIME_STEP / (2.0 * eps)
        tables.append(((1.0 - ratio) / (1.0 + ratio), TIME_STEP / eps / (1.0 + ratio)))

    def spread(z, _):
        kind = mat_ref[z].reshape(rows // 8, 8, cols)
        dec = jnp.broadcast_to(tables[0][0][None], kind.shape)
        gai = jnp.broadcast_to(tables[0][1][None], kind.shape)
        for m in range(1, len(tables)):
            hit = kind == m
            dec = jnp.where(hit, tables[m][0][None], dec)
            gai = jnp.where(hit, tables[m][1][None], gai)
        decay[z] = dec.reshape(rows, cols)
        gain[z] = gai.reshape(rows, cols)
        return 0

    lax.fori_loop(0, nz, spread, 0)
    finish_halo(0, -1)

    for z in range(nz):
        ex, ey, ez = e_ref[0, z], e_ref[1, z], e_ref[2, z]
        if z + 1 < nz:
            dz_x, dz_y = e_ref[0, z + 1] - ex, e_ref[1, z + 1] - ey
        else:
            dz_x, dz_y = -ex, -ey
        edge = xrecv[0]

        def ahead_x(comp, j):
            far = jnp.where(
                lane == cols - 1, pltpu.roll(edge, (cols - 1 - j) % cols, 1), pltpu.roll(comp, cols - 1, 1)
            )
            return far - comp

        def ahead_y(comp, j):
            halo = jnp.broadcast_to(yrecv[0, j : j + 1, :], (rows, cols))
            return jnp.where(row == rows - 1, halo, pltpu.roll(comp, rows - 1, 0)) - comp

        curl = (
            ahead_y(ez, nz + z) - dz_y,
            dz_x - ahead_x(ez, nz + z),
            ahead_x(ey, z) - ahead_y(ex, z),
        )
        for c in range(3):
            h_out[c, z] = h_ref[c, z] - TIME_STEP * curl[c]

    start_wires(0, h_out)
    filter_lines(0)
    back(0)
    merge(0, h_out)

    pack_edges(1, h_out, cols - 1, rows - 1)
    start_halo(1, 1)
    finish_halo(1, 1)

    for z in range(nz):
        hx, hy, hz = h_out[0, z], h_out[1, z], h_out[2, z]
        if z > 0:
            dz_x, dz_y = hx - h_out[0, z - 1], hy - h_out[1, z - 1]
        else:
            dz_x, dz_y = hx, hy
        edge = xrecv[1]

        def behind_x(comp, j):
            far = jnp.where(lane == 0, pltpu.roll(edge, (cols - j) % cols, 1), pltpu.roll(comp, 1, 1))
            return comp - far

        def behind_y(comp, j):
            halo = jnp.broadcast_to(yrecv[1, j : j + 1, :], (rows, cols))
            return comp - jnp.where(row == 0, halo, pltpu.roll(comp, 1, 0))

        curl = (
            behind_y(hz, nz + z) - dz_y,
            dz_x - behind_x(hz, nz + z),
            behind_x(hy, z) - behind_y(hx, z),
        )
        for c in range(3):
            e_out[c, z] = decay[z] * e_ref[c, z] + gain[z] * curl[c]

    start_wires(1, e_out)
    filter_lines(1)
    back(1)
    merge(1, e_out)
    drain(0)
    drain(1)

    @pl.when(jnp.logical_not(i_own))
    def _():
        strip_copy.wait()


def body(n_gx, n_gy, e_field, h_field, material, permittivity, conductivity, wire_layers):
    _, nz, rows, cols = e_field.shape
    n_lines = n_gy * rows
    n_wires = nz // 2
    n_planes = 3 * n_wires
    strip = jnp.asarray(filter_strip(n_lines, TILE))
    smem = pl.BlockSpec(memory_space=pltpu.SMEM)
    vmem = pl.BlockSpec(memory_space=pltpu.VMEM)
    block = jax.ShapeDtypeStruct(e_field.shape, F32)
    dma = pltpu.SemaphoreType.DMA
    return pl.pallas_call(
        functools.partial(kernel, n_gx, n_gy, n_wires),
        out_shape=(block, block),
        in_specs=[smem, smem, smem, vmem, vmem, vmem, pl.BlockSpec(memory_space=pl.ANY)],
        out_specs=(vmem, vmem),
        scratch_shapes=[
            pltpu.VMEM(strip.shape, BF16),
            pltpu.VMEM((2, rows, cols), F32),
            pltpu.VMEM((2, rows, cols), F32),
            pltpu.VMEM((2, 2 * nz, cols), F32),
            pltpu.VMEM((2, 2 * nz, cols), F32),
            pltpu.VMEM((2, n_planes, rows, cols), BF16),
            pltpu.VMEM((2, n_gy, rows, cols), BF16),
            pltpu.VMEM((2, n_gy, rows, cols), F32),
            pltpu.VMEM((2, n_planes, rows, cols), F32),
            pltpu.VMEM((nz, rows, cols), F32),
            pltpu.VMEM((nz, rows, cols), F32),
            dma((2, 2)),
            dma((2, 2)),
            dma((2, n_planes)),
            dma((2, n_gy)),
            dma((2, n_gy)),
            dma((2, n_planes)),
            dma,
        ],
        compiler_params=pltpu.CompilerParams(collective_id=0, has_side_effects=True),
    )(permittivity, conductivity, wire_layers, e_field, h_field, material, strip)


def solution(mesh):
    field = P(None, None, "gy", "gx")
    placed = (field, field, P(None, "gy", "gx"), P(), P(), P())
    return jax.shard_map(
        functools.partial(body, mesh.shape["gx"], mesh.shape["gy"]),
        mesh=mesh,
        in_specs=placed,
        out_specs=(field, field),
        check_vma=False,
    )
```

```python
import functools
import math

import jax
import jax.numpy as jnp
import ml_dtypes
import numpy as np
from jax import lax
from jax.experimental import pallas as pl
from jax.experimental.pallas import tpu as pltpu
from jax.sharding import PartitionSpec as P

TIME_STEP = 0.9
MESH = pl.DeviceIdType.MESH
F32 = jnp.float32
BF16 = jnp.bfloat16
TILE = 256


def filter_strip(n_cols, tile):
    row_pos = np.arange(tile, dtype=np.int64)[:, None]
    col_pos = np.arange(2 * n_cols - tile, dtype=np.int64)[None, :]
    delta = row_pos - col_pos + (n_cols - tile)
    modes = 2 * (n_cols // 4) + 1
    turned = np.mod(modes * delta, 2 * n_cols)
    safe_delta = np.where(delta == 0, 1, delta)
    pi = np.float32(math.pi)
    upper = np.sin(pi * turned.astype(np.float32) / np.float32(n_cols))
    lower = np.float32(n_cols) * np.sin(pi * safe_delta.astype(np.float32) / np.float32(n_cols))
    band = np.where(delta == 0, np.float32(modes / n_cols), upper / lower)
    out = np.float32(0.7) * band + np.where(delta == 0, np.float32(0.3), np.float32(0.0))
    return out.astype(np.float32).astype(ml_dtypes.bfloat16)


def owner_on(chip):
    return chip * 2 + (chip + chip // 4) % 2


def plane_of(chip):
    return chip // 4 * 3 + (chip % 4 + 2) % 3


def giver_of(plane, gy):
    far = gy // 4 % 2
    spot = plane % 3
    z = jnp.where(spot == 2, 3 * far, spot + 1)
    return owner_on(plane // 3 * 4 + z)


def kernel(
    n_gx, n_gy, n_wires,
    eps_ref, sig_ref, wire_ref, e_hbm, h_hbm, mat_hbm, strip_hbm,
    e_hbm_out, h_hbm_out,
    e_ref, h_ref, mat_ref, e_out, h_out, strip, xsend, xrecv, ysend, yrecv, wires, lines, res, filt, decay, gain,
    halo_send, halo_recv, wire_send, line_recv, res_send, ret_recv, strip_sem, in_sem, out_sem,
):
    _, nz, rows, cols = e_ref.shape
    n_planes = 3 * n_wires
    n_lines = n_gy * rows
    blocks = n_lines // TILE
    per_block = TILE // rows
    gx = lax.axis_index("gx")
    gy = lax.axis_index("gy")

    n_chips = n_gy // 2
    inputs = [
        pltpu.make_async_copy(src, dst, in_sem.at[i])
        for i, (src, dst) in enumerate(((e_hbm, e_ref), (h_hbm, h_ref), (mat_hbm, mat_ref)))
    ]
    for copy in inputs:
        copy.start()

    barrier = pltpu.get_barrier_semaphore()
    for step in (1, n_gx - 1):
        pl.semaphore_signal(
            barrier, inc=1, device_id={"gx": lax.rem(gx + step, n_gx)}, device_id_type=MESH
        )

    def greet(k, _):
        pl.semaphore_signal(
            barrier, inc=1, device_id={"gy": lax.rem(gy + k, n_gy)}, device_id_type=MESH
        )
        return 0

    lax.fori_loop(1, n_gy, greet, 0)

    strip_copy = pltpu.make_async_copy(strip_hbm, strip, strip_sem)
    strip_copy.start()

    lane = lax.broadcasted_iota(jnp.int32, (rows, cols), 1)
    row = lax.broadcasted_iota(jnp.int32, (rows, cols), 0)

    is_wire = [wire_ref[z] for z in range(nz)]
    rank, layer_of, seen = [], [jnp.int32(0)] * n_wires, jnp.int32(0)
    for z in range(nz):
        rank.append(jnp.minimum(seen, n_wires - 1))
        for k in range(n_wires):
            layer_of[k] = layer_of[k] + jnp.where((is_wire[z] == 1) & (seen == k), z, 0)
        seen = seen + is_wire[z]

    def pack_edges(phase, src, col, edge_row):
        total = jnp.zeros((rows, cols), F32)
        for c in (1, 2):
            for z in range(nz):
                j = (c - 1) * nz + z
                moved = pltpu.roll(src[c, z], (j - col) % cols, 1)
                total = jnp.where(lane == j, moved, total)
        xsend[phase] = total
        for i, c in enumerate((0, 2)):
            for z in range(nz):
                ysend[phase, i * nz + z : i * nz + z + 1, :] = src[c, z, edge_row : edge_row + 1, :]

    def halo_copies(phase, step):
        x_copy = pltpu.make_async_remote_copy(
            src_ref=xsend.at[phase],
            dst_ref=xrecv.at[phase],
            send_sem=halo_send.at[phase, 0],
            recv_sem=halo_recv.at[phase, 0],
            device_id={"gx": lax.rem(gx + step + n_gx, n_gx)},
            device_id_type=MESH,
        )
        y_copy = pltpu.make_async_remote_copy(
            src_ref=ysend.at[phase],
            dst_ref=yrecv.at[phase],
            send_sem=halo_send.at[phase, 1],
            recv_sem=halo_recv.at[phase, 1],
            device_id={"gy": lax.rem(gy + step + n_gy, n_gy)},
            device_id_type=MESH,
        )
        return x_copy, y_copy

    def start_halo(phase, step):
        x_copy, y_copy = halo_copies(phase, step)
        x_copy.start()
        sender = gy > 0 if step < 0 else gy < n_gy - 1

        @pl.when(sender)
        def _():
            y_copy.start()

    def finish_halo(phase, step):
        x_copy, y_copy = halo_copies(phase, step)
        x_copy.wait()
        sender = gy > 0 if step < 0 else gy < n_gy - 1
        receiver = gy < n_gy - 1 if step < 0 else gy > 0

        @pl.when(sender)
        def _():
            y_copy.wait_send()

        @pl.when(receiver)
        def _():
            y_copy.wait_recv()

    def start_wires(phase, src):
        for c in range(3):
            for k in range(n_wires):
                wires[phase, c * n_wires + k] = src[c, layer_of[k]].astype(BF16)

        def send(t, _):
            to = lax.rem(t + gy // 2, n_chips)
            plane = plane_of(to)
            owner = owner_on(to)

            @pl.when(owner != gy)
            def _():
                pltpu.make_async_remote_copy(
                    src_ref=wires.at[phase, plane],
                    dst_ref=lines.at[phase, gy],
                    send_sem=wire_send.at[phase, to],
                    recv_sem=line_recv.at[phase, gy],
                    device_id={"gy": owner},
                    device_id_type=MESH,
                ).start()

            @pl.when(owner == gy)
            def _():
                pltpu.make_async_copy(
                    wires.at[phase, plane], lines.at[phase, gy], line_recv.at[phase, gy]
                ).start()

            return 0

        lax.fori_loop(0, n_chips, send, 0)

    chip = gy // 2
    my_plane = plane_of(chip)
    i_own = owner_on(chip) == gy
    depth = chip % 4

    def serves(at):
        return (depth == 1) | (depth == 2) | (depth // 2 == at % 2)

    def filter_lines(phase):
        @pl.when(i_own)
        def _():
            def arrive(s, _):
                @pl.when(s != gy)
                def _():
                    pltpu.make_async_remote_copy(
                        src_ref=wires.at[phase, my_plane],
                        dst_ref=lines.at[phase, s],
                        send_sem=wire_send.at[phase, 0],
                        recv_sem=line_recv.at[phase, s],
                        device_id={"gy": s},
                        device_id_type=MESH,
                    ).wait_recv()

                @pl.when(s == gy)
                def _():
                    pltpu.make_async_copy(
                        wires.at[phase, my_plane], lines.at[phase, s], line_recv.at[phase, s]
                    ).wait()

                return 0

            lax.fori_loop(0, n_gy, arrive, 0)
            if phase == 0:
                strip_copy.wait()

            def block(t, _):
                at = lax.rem(t + chip // 2, blocks)

                @pl.when(serves(at))
                def _():
                    start = pl.multiple_of((blocks - 1 - at) * TILE, TILE)
                    out = jnp.dot(
                        strip[:, pl.ds(start, n_lines)],
                        lines[phase].reshape(n_lines, cols),
                        preferred_element_type=F32,
                    )
                    res[phase, pl.ds(at * per_block, per_block)] = out.reshape(per_block, rows, cols)

                    def give(i, _):
                        to = at * per_block + i

                        @pl.when(to != gy)
                        def _():
                            pltpu.make_async_remote_copy(
                                src_ref=res.at[phase, to],
                                dst_ref=filt.at[phase, my_plane],
                                send_sem=res_send.at[phase, to],
                                recv_sem=ret_recv.at[phase, my_plane],
                                device_id={"gy": to},
                                device_id_type=MESH,
                            ).start()

                        @pl.when(to == gy)
                        def _():
                            pltpu.make_async_copy(
                                res.at[phase, to], filt.at[phase, my_plane], ret_recv.at[phase, my_plane]
                            ).start()

                        return 0

                    lax.fori_loop(0, per_block, give, 0)
                return 0


            lax.fori_loop(0, blocks, block, 0)

    def back(phase):
        def arrive(plane, _):
            owner = giver_of(plane, gy)

            @pl.when(owner != gy)
            def _():
                pltpu.make_async_remote_copy(
                    src_ref=res.at[phase, gy],
                    dst_ref=filt.at[phase, plane],
                    send_sem=res_send.at[phase, gy],
                    recv_sem=ret_recv.at[phase, plane],
                    device_id={"gy": owner},
                    device_id_type=MESH,
                ).wait_recv()

            @pl.when(owner == gy)
            def _():
                pltpu.make_async_copy(
                    res.at[phase, gy], filt.at[phase, plane], ret_recv.at[phase, plane]
                ).wait()

            return 0

        lax.fori_loop(0, n_planes, arrive, 0)

    def drain(phase):
        def wire_gone(to, _):
            owner = owner_on(to)

            @pl.when(owner != gy)
            def _():
                pltpu.make_async_remote_copy(
                    src_ref=wires.at[phase, plane_of(to)],
                    dst_ref=lines.at[phase, gy],
                    send_sem=wire_send.at[phase, to],
                    recv_sem=line_recv.at[phase, gy],
                    device_id={"gy": owner},
                    device_id_type=MESH,
                ).wait_send()

            return 0

        lax.fori_loop(0, n_chips, wire_gone, 0)

        @pl.when(i_own)
        def _():
            def row_gone(to, _):
                @pl.when((to != gy) & serves(to // per_block))
                def _():
                    pltpu.make_async_remote_copy(
                        src_ref=res.at[phase, to],
                        dst_ref=filt.at[phase, my_plane],
                        send_sem=res_send.at[phase, to],
                        recv_sem=ret_recv.at[phase, my_plane],
                        device_id={"gy": to},
                        device_id_type=MESH,
                    ).wait_send()

                return 0

            lax.fori_loop(0, n_gy, row_gone, 0)

    def merge(phase, dst):
        for z in range(nz):
            chosen = jnp.full((rows, cols), is_wire[z], jnp.int32) == 1
            for c in range(3):
                dst[c, z] = jnp.where(chosen, filt[phase, c * n_wires + rank[z]], dst[c, z])

    results = (
        pltpu.make_async_copy(h_out, h_hbm_out, out_sem.at[0]),
        pltpu.make_async_copy(e_out, e_hbm_out, out_sem.at[1]),
    )

    inputs[0].wait()
    pack_edges(0, e_ref, 0, 0)

    @pl.when(gy == n_gy - 1)
    def _():
        yrecv[0] = jnp.zeros((2 * nz, cols), F32)

    @pl.when(gy == 0)
    def _():
        yrecv[1] = jnp.zeros((2 * nz, cols), F32)

    pl.semaphore_wait(barrier, n_gy + 1)
    start_halo(0, -1)

    inputs[1].wait()
    inputs[2].wait()
    tables = []
    for m in range(eps_ref.shape[0]):
        eps = jnp.full((8, cols), eps_ref[m], F32)
        ratio = jnp.full((8, cols), sig_ref[m], F32) * TIME_STEP / (2.0 * eps)
        tables.append(((1.0 - ratio) / (1.0 + ratio), TIME_STEP / eps / (1.0 + ratio)))

    def spread(z, _):
        kind = mat_ref[z].reshape(rows // 8, 8, cols)
        dec = jnp.broadcast_to(tables[0][0][None], kind.shape)
        gai = jnp.broadcast_to(tables[0][1][None], kind.shape)
        for m in range(1, len(tables)):
            hit = kind == m
            dec = jnp.where(hit, tables[m][0][None], dec)
            gai = jnp.where(hit, tables[m][1][None], gai)
        decay[z] = dec.reshape(rows, cols)
        gain[z] = gai.reshape(rows, cols)
        return 0

    lax.fori_loop(0, nz, spread, 0)
    finish_halo(0, -1)

    for z in range(nz):
        ex, ey, ez = e_ref[0, z], e_ref[1, z], e_ref[2, z]
        if z + 1 < nz:
            dz_x, dz_y = e_ref[0, z + 1] - ex, e_ref[1, z + 1] - ey
        else:
            dz_x, dz_y = -ex, -ey
        edge = xrecv[0]

        def ahead_x(comp, j):
            far = jnp.where(
                lane == cols - 1, pltpu.roll(edge, (cols - 1 - j) % cols, 1), pltpu.roll(comp, cols - 1, 1)
            )
            return far - comp

        def ahead_y(comp, j):
            halo = jnp.broadcast_to(yrecv[0, j : j + 1, :], (rows, cols))
            return jnp.where(row == rows - 1, halo, pltpu.roll(comp, rows - 1, 0)) - comp

        curl = (
            ahead_y(ez, nz + z) - dz_y,
            dz_x - ahead_x(ez, nz + z),
            ahead_x(ey, z) - ahead_y(ex, z),
        )
        for c in range(3):
            h_out[c, z] = h_ref[c, z] - TIME_STEP * curl[c]

    start_wires(0, h_out)
    filter_lines(0)
    back(0)
    merge(0, h_out)

    pack_edges(1, h_out, cols - 1, rows - 1)
    start_halo(1, 1)
    results[0].start()
    finish_halo(1, 1)

    for z in range(nz):
        hx, hy, hz = h_out[0, z], h_out[1, z], h_out[2, z]
        if z > 0:
            dz_x, dz_y = hx - h_out[0, z - 1], hy - h_out[1, z - 1]
        else:
            dz_x, dz_y = hx, hy
        edge = xrecv[1]

        def behind_x(comp, j):
            far = jnp.where(lane == 0, pltpu.roll(edge, (cols - j) % cols, 1), pltpu.roll(comp, 1, 1))
            return comp - far

        def behind_y(comp, j):
            halo = jnp.broadcast_to(yrecv[1, j : j + 1, :], (rows, cols))
            return comp - jnp.where(row == 0, halo, pltpu.roll(comp, 1, 0))

        curl = (
            behind_y(hz, nz + z) - dz_y,
            dz_x - behind_x(hz, nz + z),
            behind_x(hy, z) - behind_y(hx, z),
        )
        for c in range(3):
            e_out[c, z] = decay[z] * e_ref[c, z] + gain[z] * curl[c]

    start_wires(1, e_out)
    filter_lines(1)
    back(1)
    merge(1, e_out)
    results[1].start()
    drain(0)
    drain(1)

    @pl.when(jnp.logical_not(i_own))
    def _():
        strip_copy.wait()

    for copy in results:
        copy.wait()


def body(n_gx, n_gy, e_field, h_field, material, permittivity, conductivity, wire_layers):
    _, nz, rows, cols = e_field.shape
    n_lines = n_gy * rows
    n_wires = nz // 2
    n_planes = 3 * n_wires
    strip = jnp.asarray(filter_strip(n_lines, TILE))
    smem = pl.BlockSpec(memory_space=pltpu.SMEM)
    hbm = pl.BlockSpec(memory_space=pl.ANY)
    block = jax.ShapeDtypeStruct(e_field.shape, F32)
    dma = pltpu.SemaphoreType.DMA
    return pl.pallas_call(
        functools.partial(kernel, n_gx, n_gy, n_wires),
        out_shape=(block, block),
        in_specs=[smem, smem, smem, hbm, hbm, hbm, hbm],
        out_specs=(hbm, hbm),
        scratch_shapes=[
            pltpu.VMEM(e_field.shape, F32),
            pltpu.VMEM(h_field.shape, F32),
            pltpu.VMEM(material.shape, jnp.int32),
            pltpu.VMEM(e_field.shape, F32),
            pltpu.VMEM(h_field.shape, F32),
            pltpu.VMEM(strip.shape, BF16),
            pltpu.VMEM((2, rows, cols), F32),
            pltpu.VMEM((2, rows, cols), F32),
            pltpu.VMEM((2, 2 * nz, cols), F32),
            pltpu.VMEM((2, 2 * nz, cols), F32),
            pltpu.VMEM((2, n_planes, rows, cols), BF16),
            pltpu.VMEM((2, n_gy, rows, cols), BF16),
            pltpu.VMEM((2, n_gy, rows, cols), F32),
            pltpu.VMEM((2, n_planes, rows, cols), F32),
            pltpu.VMEM((nz, rows, cols), F32),
            pltpu.VMEM((nz, rows, cols), F32),
            dma((2, 2)),
            dma((2, 2)),
            dma((2, n_gy // 2)),
            dma((2, n_gy)),
            dma((2, n_gy)),
            dma((2, n_planes)),
            dma,
            dma((3,)),
            dma((2,)),
        ],
        compiler_params=pltpu.CompilerParams(collective_id=0, has_side_effects=True),
    )(permittivity, conductivity, wire_layers, e_field, h_field, material, strip)


def solution(mesh):
    field = P(None, None, "gy", "gx")
    placed = (field, field, P(None, "gy", "gx"), P(), P(), P())
    return jax.shard_map(
        functools.partial(body, mesh.shape["gx"], mesh.shape["gy"]),
        mesh=mesh,
        in_specs=placed,
        out_specs=(field, field),
        check_vma=False,
    )
```

```python
import functools
import math

import jax
import jax.numpy as jnp
import ml_dtypes
import numpy as np
from jax import lax
from jax.experimental import pallas as pl
from jax.experimental.pallas import tpu as pltpu
from jax.sharding import PartitionSpec as P

TIME_STEP = 0.9
MESH = pl.DeviceIdType.MESH
F32 = jnp.float32
BF16 = jnp.bfloat16
TILE = 256


def filter_strip(n_cols, tile):
    row_pos = np.arange(tile, dtype=np.int64)[:, None]
    col_pos = np.arange(2 * n_cols - tile, dtype=np.int64)[None, :]
    delta = row_pos - col_pos + (n_cols - tile)
    modes = 2 * (n_cols // 4) + 1
    turned = np.mod(modes * delta, 2 * n_cols)
    safe_delta = np.where(delta == 0, 1, delta)
    pi = np.float32(math.pi)
    upper = np.sin(pi * turned.astype(np.float32) / np.float32(n_cols))
    lower = np.float32(n_cols) * np.sin(pi * safe_delta.astype(np.float32) / np.float32(n_cols))
    band = np.where(delta == 0, np.float32(modes / n_cols), upper / lower)
    out = np.float32(0.7) * band + np.where(delta == 0, np.float32(0.3), np.float32(0.0))
    return out.astype(np.float32).astype(ml_dtypes.bfloat16)


def owner_on(chip):
    return chip * 2 + (chip + chip // 4) % 2


def plane_of(chip):
    return chip // 4 * 3 + (chip % 4 + 2) % 3


def edge_owner(level):
    return (level * 5) * 2 + 1


def giver_of(plane, gy):
    far = gy // 4 % 2
    spot = plane % 3
    z = jnp.where(spot == 2, 3 * far, spot + 1)
    return owner_on(plane // 3 * 4 + z)


def kernel(
    n_gx, n_gy, n_wires,
    eps_ref, sig_ref, wire_ref, e_hbm, h_hbm, mat_hbm, strip_hbm,
    e_hbm_out, h_hbm_out,
    e_ref, h_ref, mat_ref, e_out, h_out, strip, xsend, xrecv, ysend, yrecv, wires, lines, res, filt, decay, gain,
    edge_low, edge_lines, edge_res, edge_filt, tails,
    halo_send, halo_recv, wire_send, line_recv, res_send, ret_recv, strip_sem, in_sem, out_sem,
    edge_send, edge_recv, edge_give, edge_back, tail_send, tail_recv,
):
    _, nz, rows, cols = e_ref.shape
    n_planes = 3 * n_wires
    n_lines = n_gy * rows
    blocks = n_lines // TILE
    per_block = TILE // rows
    gx = lax.axis_index("gx")
    gy = lax.axis_index("gy")

    n_chips = n_gy // 2
    inputs = [
        pltpu.make_async_copy(src, dst, in_sem.at[i])
        for i, (src, dst) in enumerate(((e_hbm, e_ref), (h_hbm, h_ref), (mat_hbm, mat_ref)))
    ]
    for copy in inputs:
        copy.start()

    barrier = pltpu.get_barrier_semaphore()
    for step in (1, n_gx - 1):
        pl.semaphore_signal(
            barrier, inc=1, device_id={"gx": lax.rem(gx + step, n_gx)}, device_id_type=MESH
        )

    def greet(k, _):
        pl.semaphore_signal(
            barrier, inc=1, device_id={"gy": lax.rem(gy + k, n_gy)}, device_id_type=MESH
        )
        return 0

    lax.fori_loop(1, n_gy, greet, 0)

    strip_copy = pltpu.make_async_copy(strip_hbm, strip, strip_sem)
    strip_copy.start()

    lane = lax.broadcasted_iota(jnp.int32, (rows, cols), 1)
    row = lax.broadcasted_iota(jnp.int32, (rows, cols), 0)

    is_wire = [wire_ref[z] for z in range(nz)]
    rank, layer_of, seen = [], [jnp.int32(0)] * n_wires, jnp.int32(0)
    for z in range(nz):
        rank.append(jnp.minimum(seen, n_wires - 1))
        for k in range(n_wires):
            layer_of[k] = layer_of[k] + jnp.where((is_wire[z] == 1) & (seen == k), z, 0)
        seen = seen + is_wire[z]

    def pack_edges(phase, src, col, edge_row):
        total = jnp.zeros((rows, cols), F32)
        for c in (1, 2):
            for z in range(nz):
                j = (c - 1) * nz + z
                moved = pltpu.roll(src[c, z], (j - col) % cols, 1)
                total = jnp.where(lane == j, moved, total)
        xsend[phase] = total
        for i, c in enumerate((0, 2)):
            for z in range(nz):
                ysend[phase, i * nz + z : i * nz + z + 1, :] = src[c, z, edge_row : edge_row + 1, :]

    def halo_copies(phase, step):
        x_copy = pltpu.make_async_remote_copy(
            src_ref=xsend.at[phase],
            dst_ref=xrecv.at[phase],
            send_sem=halo_send.at[phase, 0],
            recv_sem=halo_recv.at[phase, 0],
            device_id={"gx": lax.rem(gx + step + n_gx, n_gx)},
            device_id_type=MESH,
        )
        y_copy = pltpu.make_async_remote_copy(
            src_ref=ysend.at[phase],
            dst_ref=yrecv.at[phase],
            send_sem=halo_send.at[phase, 1],
            recv_sem=halo_recv.at[phase, 1],
            device_id={"gy": lax.rem(gy + step + n_gy, n_gy)},
            device_id_type=MESH,
        )
        return x_copy, y_copy

    def start_halo(phase, step):
        x_copy, y_copy = halo_copies(phase, step)
        x_copy.start()
        sender = gy > 0 if step < 0 else gy < n_gy - 1

        @pl.when(sender)
        def _():
            y_copy.start()

    def finish_halo(phase, step):
        x_copy, y_copy = halo_copies(phase, step)
        x_copy.wait()
        sender = gy > 0 if step < 0 else gy < n_gy - 1
        receiver = gy < n_gy - 1 if step < 0 else gy > 0

        @pl.when(sender)
        def _():
            y_copy.wait_send()

        @pl.when(receiver)
        def _():
            y_copy.wait_recv()

    def start_wires(phase, src):
        for c in range(3):
            for k in range(n_wires):
                wires[phase, c * n_wires + k] = src[c, layer_of[k]].astype(BF16)

        def send(t, _):
            to = lax.rem(t + gy // 2, n_chips)
            plane = plane_of(to)
            owner = owner_on(to)

            @pl.when(owner != gy)
            def _():
                pltpu.make_async_remote_copy(
                    src_ref=wires.at[phase, plane],
                    dst_ref=lines.at[phase, gy],
                    send_sem=wire_send.at[phase, to],
                    recv_sem=line_recv.at[phase, gy],
                    device_id={"gy": owner},
                    device_id_type=MESH,
                ).start()

            @pl.when(owner == gy)
            def _():
                pltpu.make_async_copy(
                    wires.at[phase, plane], lines.at[phase, gy], line_recv.at[phase, gy]
                ).start()

            return 0

        lax.fori_loop(0, n_chips, send, 0)

    chip = gy // 2
    my_plane = plane_of(chip)
    i_own = owner_on(chip) == gy
    depth = chip % 4

    def serves(at):
        return (depth == 1) | (depth == 2) | (depth // 2 == at % 2)

    def tail_copy(plane, to):
        return pltpu.make_async_remote_copy(
            src_ref=res.at[0, to, pl.ds(rows - 8, 8)],
            dst_ref=tails.at[plane],
            send_sem=tail_send.at[to],
            recv_sem=tail_recv.at[plane],
            device_id={"gy": lax.rem(to + 1, n_gy)},
            device_id_type=MESH,
        )

    def own_tail(plane, to):
        return pltpu.make_async_copy(
            res.at[0, to, pl.ds(rows - 8, 8)], tails.at[plane], tail_recv.at[plane]
        )

    has_tails = my_plane // n_wires != 1

    def start_tail(to):
        @pl.when(has_tails & (to + 1 < n_gy) & (to + 1 != gy))
        def _():
            tail_copy(my_plane, to).start()

        @pl.when(has_tails & (to + 1 == gy))
        def _():
            own_tail(my_plane, to).start()

    level = chip % 4
    i_edge = edge_owner(level) == gy

    def edge_copy(to_level, source):
        return pltpu.make_async_remote_copy(
            src_ref=edge_low,
            dst_ref=edge_lines.at[source],
            send_sem=edge_send.at[to_level],
            recv_sem=edge_recv.at[source],
            device_id={"gy": edge_owner(to_level)},
            device_id_type=MESH,
        )

    def own_edge():
        return pltpu.make_async_copy(edge_low, edge_lines.at[gy], edge_recv.at[gy])

    def start_edges():
        edge_low[...] = xrecv[1].astype(BF16)

        def send(t, _):
            to_level = lax.rem(t + level, 4)

            @pl.when(edge_owner(to_level) != gy)
            def _():
                edge_copy(to_level, gy).start()

            @pl.when(edge_owner(to_level) == gy)
            def _():
                own_edge().start()

            return 0

        lax.fori_loop(0, 4, send, 0)

    def edge_give_copy(slot):
        return pltpu.make_async_remote_copy(
            src_ref=edge_res.at[slot],
            dst_ref=edge_filt,
            send_sem=edge_give.at[slot],
            recv_sem=edge_back,
            device_id={"gy": (slot // 2 * 4 + level) * 2 + slot % 2},
            device_id_type=MESH,
        )

    def own_edge_give(slot):
        return pltpu.make_async_copy(edge_res.at[slot], edge_filt, edge_back)

    own_slot = chip // 4 * 2 + gy % 2

    def filter_edges():
        @pl.when(i_edge)
        def _():
            def arrive(s, _):
                @pl.when(s != gy)
                def _():
                    edge_copy(level, s).wait_recv()

                @pl.when(s == gy)
                def _():
                    own_edge().wait()

                return 0

            lax.fori_loop(0, n_gy, arrive, 0)

            def block(t, _):
                run = lax.rem(t + level + 1, n_chips // 4)
                at = run * 2 + level // 2
                start = pl.multiple_of((blocks - 1 - at) * TILE, TILE)
                top = pl.multiple_of(level % 2 * (TILE // 2), TILE // 2)
                out = jnp.dot(
                    strip[pl.ds(top, TILE // 2), pl.ds(start, n_lines)],
                    edge_lines[...].reshape(n_lines, cols),
                    preferred_element_type=F32,
                )
                edge_res[pl.ds(run * 2, 2)] = out.reshape(2, rows, cols)

                def give(i, _):
                    slot = run * 2 + i

                    @pl.when(slot != own_slot)
                    def _():
                        edge_give_copy(slot).start()

                    @pl.when(slot == own_slot)
                    def _():
                        own_edge_give(slot).start()

                    return 0

                lax.fori_loop(0, 2, give, 0)
                return 0

            lax.fori_loop(0, n_chips // 4, block, 0)

    def edges_back():
        @pl.when(i_edge)
        def _():
            own_edge_give(own_slot).wait()

        @pl.when(jnp.logical_not(i_edge))
        def _():
            edge_give_copy(own_slot).wait_recv()

        @pl.when(gy > 0)
        def _():
            def arrive(t, _):
                plane = t + t // n_wires * n_wires
                giver = giver_of(plane, gy - 1)

                @pl.when(giver != gy)
                def _():
                    tail_copy(plane, gy).wait_recv()

                @pl.when(giver == gy)
                def _():
                    own_tail(plane, gy - 1).wait()

                return 0

            lax.fori_loop(0, 2 * n_wires, arrive, 0)

    def edges_gone():
        def sent(to_level, _):
            @pl.when(edge_owner(to_level) != gy)
            def _():
                edge_copy(to_level, gy).wait_send()

            return 0

        lax.fori_loop(0, 4, sent, 0)

        @pl.when(i_edge)
        def _():
            def given(slot, _):
                @pl.when(slot != own_slot)
                def _():
                    edge_give_copy(slot).wait_send()

                return 0

            lax.fori_loop(0, n_chips // 2, given, 0)

        @pl.when(i_own & has_tails)
        def _():
            def tail_gone(to, _):
                @pl.when((to + 1 != gy) & serves(to // per_block))
                def _():
                    tail_copy(my_plane, to).wait_send()

                return 0

            lax.fori_loop(0, n_gy - 1, tail_gone, 0)

    def filter_lines(phase):
        @pl.when(i_own)
        def _():
            def arrive(s, _):
                @pl.when(s != gy)
                def _():
                    pltpu.make_async_remote_copy(
                        src_ref=wires.at[phase, my_plane],
                        dst_ref=lines.at[phase, s],
                        send_sem=wire_send.at[phase, 0],
                        recv_sem=line_recv.at[phase, s],
                        device_id={"gy": s},
                        device_id_type=MESH,
                    ).wait_recv()

                @pl.when(s == gy)
                def _():
                    pltpu.make_async_copy(
                        wires.at[phase, my_plane], lines.at[phase, s], line_recv.at[phase, s]
                    ).wait()

                return 0

            lax.fori_loop(0, n_gy, arrive, 0)
            def block(t, _):
                at = lax.rem(t + chip // 2, blocks)

                @pl.when(serves(at))
                def _():
                    start = pl.multiple_of((blocks - 1 - at) * TILE, TILE)
                    out = jnp.dot(
                        strip[:, pl.ds(start, n_lines)],
                        lines[phase].reshape(n_lines, cols),
                        preferred_element_type=F32,
                    )
                    res[phase, pl.ds(at * per_block, per_block)] = out.reshape(per_block, rows, cols)

                    def give(i, _):
                        to = at * per_block + i

                        @pl.when(to != gy)
                        def _():
                            pltpu.make_async_remote_copy(
                                src_ref=res.at[phase, to],
                                dst_ref=filt.at[phase, my_plane],
                                send_sem=res_send.at[phase, to],
                                recv_sem=ret_recv.at[phase, my_plane],
                                device_id={"gy": to},
                                device_id_type=MESH,
                            ).start()

                        @pl.when(to == gy)
                        def _():
                            pltpu.make_async_copy(
                                res.at[phase, to], filt.at[phase, my_plane], ret_recv.at[phase, my_plane]
                            ).start()

                        if phase == 0:
                            start_tail(to)
                        return 0

                    lax.fori_loop(0, per_block, give, 0)
                return 0


            lax.fori_loop(0, blocks, block, 0)

    def back(phase):
        def arrive(plane, _):
            owner = giver_of(plane, gy)

            @pl.when(owner != gy)
            def _():
                pltpu.make_async_remote_copy(
                    src_ref=res.at[phase, gy],
                    dst_ref=filt.at[phase, plane],
                    send_sem=res_send.at[phase, gy],
                    recv_sem=ret_recv.at[phase, plane],
                    device_id={"gy": owner},
                    device_id_type=MESH,
                ).wait_recv()

            @pl.when(owner == gy)
            def _():
                pltpu.make_async_copy(
                    res.at[phase, gy], filt.at[phase, plane], ret_recv.at[phase, plane]
                ).wait()

            return 0

        lax.fori_loop(0, n_planes, arrive, 0)

    def drain(phase):
        def wire_gone(to, _):
            owner = owner_on(to)

            @pl.when(owner != gy)
            def _():
                pltpu.make_async_remote_copy(
                    src_ref=wires.at[phase, plane_of(to)],
                    dst_ref=lines.at[phase, gy],
                    send_sem=wire_send.at[phase, to],
                    recv_sem=line_recv.at[phase, gy],
                    device_id={"gy": owner},
                    device_id_type=MESH,
                ).wait_send()

            return 0

        lax.fori_loop(0, n_chips, wire_gone, 0)

        @pl.when(i_own)
        def _():
            def row_gone(to, _):
                @pl.when((to != gy) & serves(to // per_block))
                def _():
                    pltpu.make_async_remote_copy(
                        src_ref=res.at[phase, to],
                        dst_ref=filt.at[phase, my_plane],
                        send_sem=res_send.at[phase, to],
                        recv_sem=ret_recv.at[phase, my_plane],
                        device_id={"gy": to},
                        device_id_type=MESH,
                    ).wait_send()

                return 0

            lax.fori_loop(0, n_gy, row_gone, 0)

    def merge(phase, dst):
        for z in range(nz):
            chosen = jnp.full((rows, cols), is_wire[z], jnp.int32) == 1
            for c in range(3):
                dst[c, z] = jnp.where(chosen, filt[phase, c * n_wires + rank[z]], dst[c, z])

    results = (
        pltpu.make_async_copy(h_out, h_hbm_out, out_sem.at[0]),
        pltpu.make_async_copy(e_out, e_hbm_out, out_sem.at[1]),
    )

    inputs[0].wait()
    pack_edges(0, e_ref, 0, 0)

    @pl.when(gy == n_gy - 1)
    def _():
        yrecv[0] = jnp.zeros((2 * nz, cols), F32)

    @pl.when(gy == 0)
    def _():
        yrecv[1] = jnp.zeros((2 * nz, cols), F32)
        tails[...] = jnp.zeros(tails.shape, F32)

    pl.semaphore_wait(barrier, n_gy + 1)
    start_halo(0, -1)

    inputs[1].wait()
    inputs[2].wait()
    tables = []
    for m in range(eps_ref.shape[0]):
        eps = jnp.full((8, cols), eps_ref[m], F32)
        ratio = jnp.full((8, cols), sig_ref[m], F32) * TIME_STEP / (2.0 * eps)
        tables.append(((1.0 - ratio) / (1.0 + ratio), TIME_STEP / eps / (1.0 + ratio)))

    def spread(z, _):
        kind = mat_ref[z].reshape(rows // 8, 8, cols)
        dec = jnp.broadcast_to(tables[0][0][None], kind.shape)
        gai = jnp.broadcast_to(tables[0][1][None], kind.shape)
        for m in range(1, len(tables)):
            hit = kind == m
            dec = jnp.where(hit, tables[m][0][None], dec)
            gai = jnp.where(hit, tables[m][1][None], gai)
        decay[z] = dec.reshape(rows, cols)
        gain[z] = gai.reshape(rows, cols)
        return 0

    lax.fori_loop(0, nz, spread, 0)
    finish_halo(0, -1)

    for z in range(nz):
        ex, ey, ez = e_ref[0, z], e_ref[1, z], e_ref[2, z]
        if z + 1 < nz:
            dz_x, dz_y = e_ref[0, z + 1] - ex, e_ref[1, z + 1] - ey
        else:
            dz_x, dz_y = -ex, -ey
        edge = xrecv[0]

        def ahead_x(comp, j):
            far = jnp.where(
                lane == cols - 1, pltpu.roll(edge, (cols - 1 - j) % cols, 1), pltpu.roll(comp, cols - 1, 1)
            )
            return far - comp

        def ahead_y(comp, j):
            halo = jnp.broadcast_to(yrecv[0, j : j + 1, :], (rows, cols))
            return jnp.where(row == rows - 1, halo, pltpu.roll(comp, rows - 1, 0)) - comp

        curl = (
            ahead_y(ez, nz + z) - dz_y,
            dz_x - ahead_x(ez, nz + z),
            ahead_x(ey, z) - ahead_y(ex, z),
        )
        for c in range(3):
            h_out[c, z] = h_ref[c, z] - TIME_STEP * curl[c]

    start_wires(0, h_out)
    pack_edges(1, h_out, cols - 1, rows - 1)
    start_halo(1, 1)
    finish_halo(1, 1)
    start_edges()
    strip_copy.wait()
    filter_lines(0)
    filter_edges()
    back(0)
    merge(0, h_out)
    results[0].start()
    edges_back()

    kept = jnp.zeros((rows, cols), jnp.int32)
    for z in range(nz):
        kept = jnp.where(lane % nz == z, is_wire[z], kept)
    left = jnp.where(kept == 1, edge_filt[...], xrecv[1])

    for z in range(nz):
        hx, hy, hz = h_out[0, z], h_out[1, z], h_out[2, z]
        if z > 0:
            dz_x, dz_y = hx - h_out[0, z - 1], hy - h_out[1, z - 1]
        else:
            dz_x, dz_y = hx, hy
        def behind_x(comp, j):
            far = jnp.where(lane == 0, pltpu.roll(left, (cols - j) % cols, 1), pltpu.roll(comp, 1, 1))
            return comp - far

        def behind_y(comp, j):
            plane = (j // nz) * 2 * n_wires + rank[z]
            raw = jnp.broadcast_to(yrecv[1, j : j + 1, :], (rows, cols))
            filtered = jnp.broadcast_to(tails[plane][7:8], (rows, cols))
            halo = jnp.where(jnp.full((rows, cols), is_wire[z], jnp.int32) == 1, filtered, raw)
            return comp - jnp.where(row == 0, halo, pltpu.roll(comp, 1, 0))

        curl = (
            behind_y(hz, nz + z) - dz_y,
            dz_x - behind_x(hz, nz + z),
            behind_x(hy, z) - behind_y(hx, z),
        )
        for c in range(3):
            e_out[c, z] = decay[z] * e_ref[c, z] + gain[z] * curl[c]

    start_wires(1, e_out)
    filter_lines(1)
    back(1)
    merge(1, e_out)
    results[1].start()
    drain(0)
    edges_gone()
    drain(1)

    for copy in results:
        copy.wait()


def body(n_gx, n_gy, e_field, h_field, material, permittivity, conductivity, wire_layers):
    _, nz, rows, cols = e_field.shape
    n_lines = n_gy * rows
    n_wires = nz // 2
    n_planes = 3 * n_wires
    strip = jnp.asarray(filter_strip(n_lines, TILE))
    smem = pl.BlockSpec(memory_space=pltpu.SMEM)
    hbm = pl.BlockSpec(memory_space=pl.ANY)
    block = jax.ShapeDtypeStruct(e_field.shape, F32)
    dma = pltpu.SemaphoreType.DMA
    return pl.pallas_call(
        functools.partial(kernel, n_gx, n_gy, n_wires),
        out_shape=(block, block),
        in_specs=[smem, smem, smem, hbm, hbm, hbm, hbm],
        out_specs=(hbm, hbm),
        scratch_shapes=[
            pltpu.VMEM(e_field.shape, F32),
            pltpu.VMEM(h_field.shape, F32),
            pltpu.VMEM(material.shape, jnp.int32),
            pltpu.VMEM(e_field.shape, F32),
            pltpu.VMEM(h_field.shape, F32),
            pltpu.VMEM(strip.shape, BF16),
            pltpu.VMEM((2, rows, cols), F32),
            pltpu.VMEM((2, rows, cols), F32),
            pltpu.VMEM((2, 2 * nz, cols), F32),
            pltpu.VMEM((2, 2 * nz, cols), F32),
            pltpu.VMEM((2, n_planes, rows, cols), BF16),
            pltpu.VMEM((2, n_gy, rows, cols), BF16),
            pltpu.VMEM((2, n_gy, rows, cols), F32),
            pltpu.VMEM((2, n_planes, rows, cols), F32),
            pltpu.VMEM((nz, rows, cols), F32),
            pltpu.VMEM((nz, rows, cols), F32),
            pltpu.VMEM((rows, cols), BF16),
            pltpu.VMEM((n_gy, rows, cols), BF16),
            pltpu.VMEM((n_gy // 4, rows, cols), F32),
            pltpu.VMEM((rows, cols), F32),
            pltpu.VMEM((n_planes, 8, cols), F32),
            dma((2, 2)),
            dma((2, 2)),
            dma((2, n_gy // 2)),
            dma((2, n_gy)),
            dma((2, n_gy)),
            dma((2, n_planes)),
            dma,
            dma((3,)),
            dma((2,)),
            dma((4,)),
            dma((n_gy,)),
            dma((n_gy // 4,)),
            dma,
            dma((n_gy,)),
            dma((n_planes,)),
        ],
        compiler_params=pltpu.CompilerParams(collective_id=0, has_side_effects=True),
    )(permittivity, conductivity, wire_layers, e_field, h_field, material, strip)


def solution(mesh):
    field = P(None, None, "gy", "gx")
    placed = (field, field, P(None, "gy", "gx"), P(), P(), P())
    return jax.shard_map(
        functools.partial(body, mesh.shape["gx"], mesh.shape["gy"]),
        mesh=mesh,
        in_specs=placed,
        out_specs=(field, field),
        check_vma=False,
    )
```

```python
import functools
import math

import jax
import jax.numpy as jnp
import ml_dtypes
import numpy as np
from jax import lax
from jax.experimental import pallas as pl
from jax.experimental.pallas import tpu as pltpu
from jax.sharding import PartitionSpec as P

TIME_STEP = 0.9
MESH = pl.DeviceIdType.MESH
F32 = jnp.float32
BF16 = jnp.bfloat16
TILE = 256


def filter_strip(n_cols, tile):
    row_pos = np.arange(tile, dtype=np.int64)[:, None]
    col_pos = np.arange(2 * n_cols - tile, dtype=np.int64)[None, :]
    delta = row_pos - col_pos + (n_cols - tile)
    modes = 2 * (n_cols // 4) + 1
    turned = np.mod(modes * delta, 2 * n_cols)
    safe_delta = np.where(delta == 0, 1, delta)
    pi = np.float32(math.pi)
    upper = np.sin(pi * turned.astype(np.float32) / np.float32(n_cols))
    lower = np.float32(n_cols) * np.sin(pi * safe_delta.astype(np.float32) / np.float32(n_cols))
    band = np.where(delta == 0, np.float32(modes / n_cols), upper / lower)
    out = np.float32(0.7) * band + np.where(delta == 0, np.float32(0.3), np.float32(0.0))
    return out.astype(np.float32).astype(ml_dtypes.bfloat16)


def owner_on(chip):
    return chip * 2 + (chip + chip // 4) % 2


def plane_of(chip):
    return chip // 4 * 3 + (chip % 4 + 2) % 3


def edge_owner(level):
    return (level * 5) * 2 + 1


def giver_of(plane, gy):
    far = gy // 4 % 2
    spot = plane % 3
    z = jnp.where(spot == 2, 3 * far, spot + 1)
    return owner_on(plane // 3 * 4 + z)


def kernel(
    n_gx, n_gy, n_wires,
    eps_ref, sig_ref, wire_ref, e_hbm, h_hbm, mat_hbm, strip_hbm,
    e_hbm_out, h_hbm_out,
    e_ref, h_ref, mat_ref, e_out, h_out, strip, xsend, xrecv, ysend, yrecv, wires, lines, res, filt, decay, gain,
    edge_low, edge_lines, edge_res, edge_filt, tails,
    halo_send, halo_recv, wire_send, line_recv, res_send, ret_recv, strip_sem, in_sem, out_sem,
    edge_send, edge_recv, edge_give, edge_back, tail_send, tail_recv,
):
    _, nz, rows, cols = e_ref.shape
    n_planes = 3 * n_wires
    n_lines = n_gy * rows
    blocks = n_lines // TILE
    per_block = TILE // rows
    gx = lax.axis_index("gx")
    gy = lax.axis_index("gy")

    n_chips = n_gy // 2
    inputs = [
        pltpu.make_async_copy(src, dst, in_sem.at[i])
        for i, (src, dst) in enumerate(((e_hbm, e_ref), (h_hbm, h_ref), (mat_hbm, mat_ref)))
    ]
    for copy in inputs:
        copy.start()

    barrier = pltpu.get_barrier_semaphore()
    for step in (1, n_gx - 1):
        pl.semaphore_signal(
            barrier, inc=1, device_id={"gx": lax.rem(gx + step, n_gx)}, device_id_type=MESH
        )

    def greet(k, _):
        pl.semaphore_signal(
            barrier, inc=1, device_id={"gy": lax.rem(gy + k, n_gy)}, device_id_type=MESH
        )
        return 0

    lax.fori_loop(1, n_gy, greet, 0)

    strip_copy = pltpu.make_async_copy(strip_hbm, strip, strip_sem)
    strip_copy.start()

    lane = lax.broadcasted_iota(jnp.int32, (rows, cols), 1)
    row = lax.broadcasted_iota(jnp.int32, (rows, cols), 0)

    is_wire = [wire_ref[z] for z in range(nz)]
    rank, layer_of, seen = [], [jnp.int32(0)] * n_wires, jnp.int32(0)
    for z in range(nz):
        rank.append(jnp.minimum(seen, n_wires - 1))
        for k in range(n_wires):
            layer_of[k] = layer_of[k] + jnp.where((is_wire[z] == 1) & (seen == k), z, 0)
        seen = seen + is_wire[z]

    def pack_edges(phase, src, col, edge_row):
        total = jnp.zeros((rows, cols), F32)
        for c in (1, 2):
            for z in range(nz):
                j = (c - 1) * nz + z
                moved = pltpu.roll(src[c, z], (j - col) % cols, 1)
                total = jnp.where(lane == j, moved, total)
        xsend[phase] = total
        for i, c in enumerate((0, 2)):
            for z in range(nz):
                ysend[phase, i * nz + z : i * nz + z + 1, :] = src[c, z, edge_row : edge_row + 1, :]

    def halo_copies(phase, step):
        x_copy = pltpu.make_async_remote_copy(
            src_ref=xsend.at[phase],
            dst_ref=xrecv.at[phase],
            send_sem=halo_send.at[phase, 0],
            recv_sem=halo_recv.at[phase, 0],
            device_id={"gx": lax.rem(gx + step + n_gx, n_gx)},
            device_id_type=MESH,
        )
        y_copy = pltpu.make_async_remote_copy(
            src_ref=ysend.at[phase],
            dst_ref=yrecv.at[phase],
            send_sem=halo_send.at[phase, 1],
            recv_sem=halo_recv.at[phase, 1],
            device_id={"gy": lax.rem(gy + step + n_gy, n_gy)},
            device_id_type=MESH,
        )
        return x_copy, y_copy

    def start_halo(phase, step):
        x_copy, y_copy = halo_copies(phase, step)
        x_copy.start()
        sender = gy > 0 if step < 0 else gy < n_gy - 1

        @pl.when(sender)
        def _():
            y_copy.start()

    def finish_halo(phase, step):
        x_copy, y_copy = halo_copies(phase, step)
        x_copy.wait()
        sender = gy > 0 if step < 0 else gy < n_gy - 1
        receiver = gy < n_gy - 1 if step < 0 else gy > 0

        @pl.when(sender)
        def _():
            y_copy.wait_send()

        @pl.when(receiver)
        def _():
            y_copy.wait_recv()

    def start_wires(phase, src):
        for c in range(3):
            for k in range(n_wires):
                wires[phase, c * n_wires + k] = src[c, layer_of[k]].astype(BF16)

        def send(t, _):
            to = lax.rem(t + 4 + gy // 2, n_chips)
            plane = plane_of(to)
            owner = owner_on(to)

            @pl.when(owner != gy)
            def _():
                pltpu.make_async_remote_copy(
                    src_ref=wires.at[phase, plane],
                    dst_ref=lines.at[phase, gy],
                    send_sem=wire_send.at[phase, to],
                    recv_sem=line_recv.at[phase, gy],
                    device_id={"gy": owner},
                    device_id_type=MESH,
                ).start()

            @pl.when(owner == gy)
            def _():
                pltpu.make_async_copy(
                    wires.at[phase, plane], lines.at[phase, gy], line_recv.at[phase, gy]
                ).start()

            return 0

        lax.fori_loop(0, n_chips, send, 0)

    chip = gy // 2
    my_plane = plane_of(chip)
    i_own = owner_on(chip) == gy
    depth = chip % 4

    def serves(at):
        return (depth == 1) | (depth == 2) | (depth // 2 == at % 2)

    def tail_copy(plane, to):
        return pltpu.make_async_remote_copy(
            src_ref=res.at[0, to, pl.ds(rows - 8, 8)],
            dst_ref=tails.at[plane],
            send_sem=tail_send.at[to],
            recv_sem=tail_recv.at[plane],
            device_id={"gy": lax.rem(to + 1, n_gy)},
            device_id_type=MESH,
        )

    def own_tail(plane, to):
        return pltpu.make_async_copy(
            res.at[0, to, pl.ds(rows - 8, 8)], tails.at[plane], tail_recv.at[plane]
        )

    has_tails = my_plane // n_wires != 1

    def start_tail(to):
        @pl.when(has_tails & (to + 1 < n_gy) & (to + 1 != gy))
        def _():
            tail_copy(my_plane, to).start()

        @pl.when(has_tails & (to + 1 == gy))
        def _():
            own_tail(my_plane, to).start()

    level = chip % 4
    i_edge = edge_owner(level) == gy

    def edge_copy(to_level, source):
        return pltpu.make_async_remote_copy(
            src_ref=edge_low,
            dst_ref=edge_lines.at[source],
            send_sem=edge_send.at[to_level],
            recv_sem=edge_recv.at[source],
            device_id={"gy": edge_owner(to_level)},
            device_id_type=MESH,
        )

    def own_edge():
        return pltpu.make_async_copy(edge_low, edge_lines.at[gy], edge_recv.at[gy])

    def start_edges():
        edge_low[...] = xrecv[1].astype(BF16)

        def send(t, _):
            to_level = lax.rem(t + level, 4)

            @pl.when(edge_owner(to_level) != gy)
            def _():
                edge_copy(to_level, gy).start()

            @pl.when(edge_owner(to_level) == gy)
            def _():
                own_edge().start()

            return 0

        lax.fori_loop(0, 4, send, 0)

    def edge_give_copy(slot):
        return pltpu.make_async_remote_copy(
            src_ref=edge_res.at[slot],
            dst_ref=edge_filt,
            send_sem=edge_give.at[slot],
            recv_sem=edge_back,
            device_id={"gy": (slot // 2 * 4 + level) * 2 + slot % 2},
            device_id_type=MESH,
        )

    def own_edge_give(slot):
        return pltpu.make_async_copy(edge_res.at[slot], edge_filt, edge_back)

    own_slot = chip // 4 * 2 + gy % 2

    def filter_edges():
        @pl.when(i_edge)
        def _():
            def arrive(s, _):
                @pl.when(s != gy)
                def _():
                    edge_copy(level, s).wait_recv()

                @pl.when(s == gy)
                def _():
                    own_edge().wait()

                return 0

            lax.fori_loop(0, n_gy, arrive, 0)

            def block(t, _):
                run = lax.rem(t + level + 1, n_chips // 4)
                at = run * 2 + level // 2
                start = pl.multiple_of((blocks - 1 - at) * TILE, TILE)
                top = pl.multiple_of(level % 2 * (TILE // 2), TILE // 2)
                out = jnp.dot(
                    strip[pl.ds(top, TILE // 2), pl.ds(start, n_lines)],
                    edge_lines[...].reshape(n_lines, cols),
                    preferred_element_type=F32,
                )
                edge_res[pl.ds(run * 2, 2)] = out.reshape(2, rows, cols)

                def give(i, _):
                    slot = run * 2 + i

                    @pl.when(slot != own_slot)
                    def _():
                        edge_give_copy(slot).start()

                    @pl.when(slot == own_slot)
                    def _():
                        own_edge_give(slot).start()

                    return 0

                lax.fori_loop(0, 2, give, 0)
                return 0

            lax.fori_loop(0, n_chips // 4, block, 0)

    def edges_back():
        @pl.when(i_edge)
        def _():
            own_edge_give(own_slot).wait()

        @pl.when(jnp.logical_not(i_edge))
        def _():
            edge_give_copy(own_slot).wait_recv()

        @pl.when(gy > 0)
        def _():
            def arrive(t, _):
                plane = t + t // n_wires * n_wires
                giver = giver_of(plane, gy - 1)

                @pl.when(giver != gy)
                def _():
                    tail_copy(plane, gy).wait_recv()

                @pl.when(giver == gy)
                def _():
                    own_tail(plane, gy - 1).wait()

                return 0

            lax.fori_loop(0, 2 * n_wires, arrive, 0)

    def edges_gone():
        def sent(to_level, _):
            @pl.when(edge_owner(to_level) != gy)
            def _():
                edge_copy(to_level, gy).wait_send()

            return 0

        lax.fori_loop(0, 4, sent, 0)

        @pl.when(i_edge)
        def _():
            def given(slot, _):
                @pl.when(slot != own_slot)
                def _():
                    edge_give_copy(slot).wait_send()

                return 0

            lax.fori_loop(0, n_chips // 2, given, 0)

        @pl.when(i_own & has_tails)
        def _():
            def tail_gone(to, _):
                @pl.when((to + 1 != gy) & serves(to // per_block))
                def _():
                    tail_copy(my_plane, to).wait_send()

                return 0

            lax.fori_loop(0, n_gy - 1, tail_gone, 0)

    def filter_lines(phase):
        @pl.when(i_own)
        def _():
            def arrive(s, _):
                @pl.when(s != gy)
                def _():
                    pltpu.make_async_remote_copy(
                        src_ref=wires.at[phase, my_plane],
                        dst_ref=lines.at[phase, s],
                        send_sem=wire_send.at[phase, 0],
                        recv_sem=line_recv.at[phase, s],
                        device_id={"gy": s},
                        device_id_type=MESH,
                    ).wait_recv()

                @pl.when(s == gy)
                def _():
                    pltpu.make_async_copy(
                        wires.at[phase, my_plane], lines.at[phase, s], line_recv.at[phase, s]
                    ).wait()

                return 0

            lax.fori_loop(0, n_gy, arrive, 0)
            def block(t, _):
                at = lax.rem(t + chip // 2, blocks)

                @pl.when(serves(at))
                def _():
                    start = pl.multiple_of((blocks - 1 - at) * TILE, TILE)
                    out = jnp.dot(
                        strip[:, pl.ds(start, n_lines)],
                        lines[phase].reshape(n_lines, cols),
                        preferred_element_type=F32,
                    )
                    res[phase, pl.ds(at * per_block, per_block)] = out.reshape(per_block, rows, cols)

                    def give(i, _):
                        to = at * per_block + i

                        @pl.when(to != gy)
                        def _():
                            pltpu.make_async_remote_copy(
                                src_ref=res.at[phase, to],
                                dst_ref=filt.at[phase, my_plane],
                                send_sem=res_send.at[phase, to],
                                recv_sem=ret_recv.at[phase, my_plane],
                                device_id={"gy": to},
                                device_id_type=MESH,
                            ).start()

                        @pl.when(to == gy)
                        def _():
                            pltpu.make_async_copy(
                                res.at[phase, to], filt.at[phase, my_plane], ret_recv.at[phase, my_plane]
                            ).start()

                        if phase == 0:
                            start_tail(to)
                        return 0

                    lax.fori_loop(0, per_block, give, 0)
                return 0


            lax.fori_loop(0, blocks, block, 0)

    def back(phase):
        def arrive(plane, _):
            owner = giver_of(plane, gy)

            @pl.when(owner != gy)
            def _():
                pltpu.make_async_remote_copy(
                    src_ref=res.at[phase, gy],
                    dst_ref=filt.at[phase, plane],
                    send_sem=res_send.at[phase, gy],
                    recv_sem=ret_recv.at[phase, plane],
                    device_id={"gy": owner},
                    device_id_type=MESH,
                ).wait_recv()

            @pl.when(owner == gy)
            def _():
                pltpu.make_async_copy(
                    res.at[phase, gy], filt.at[phase, plane], ret_recv.at[phase, plane]
                ).wait()

            return 0

        lax.fori_loop(0, n_planes, arrive, 0)

    def drain(phase):
        def wire_gone(to, _):
            owner = owner_on(to)

            @pl.when(owner != gy)
            def _():
                pltpu.make_async_remote_copy(
                    src_ref=wires.at[phase, plane_of(to)],
                    dst_ref=lines.at[phase, gy],
                    send_sem=wire_send.at[phase, to],
                    recv_sem=line_recv.at[phase, gy],
                    device_id={"gy": owner},
                    device_id_type=MESH,
                ).wait_send()

            return 0

        lax.fori_loop(0, n_chips, wire_gone, 0)

        @pl.when(i_own)
        def _():
            def row_gone(to, _):
                @pl.when((to != gy) & serves(to // per_block))
                def _():
                    pltpu.make_async_remote_copy(
                        src_ref=res.at[phase, to],
                        dst_ref=filt.at[phase, my_plane],
                        send_sem=res_send.at[phase, to],
                        recv_sem=ret_recv.at[phase, my_plane],
                        device_id={"gy": to},
                        device_id_type=MESH,
                    ).wait_send()

                return 0

            lax.fori_loop(0, n_gy, row_gone, 0)

    def merge(phase, dst):
        for z in range(nz):
            chosen = jnp.full((rows, cols), is_wire[z], jnp.int32) == 1
            for c in range(3):
                dst[c, z] = jnp.where(chosen, filt[phase, c * n_wires + rank[z]], dst[c, z])

    results = (
        pltpu.make_async_copy(h_out, h_hbm_out, out_sem.at[0]),
        pltpu.make_async_copy(e_out, e_hbm_out, out_sem.at[1]),
    )

    inputs[0].wait()
    pack_edges(0, e_ref, 0, 0)

    @pl.when(gy == n_gy - 1)
    def _():
        yrecv[0] = jnp.zeros((2 * nz, cols), F32)

    @pl.when(gy == 0)
    def _():
        yrecv[1] = jnp.zeros((2 * nz, cols), F32)
        tails[...] = jnp.zeros(tails.shape, F32)

    pl.semaphore_wait(barrier, n_gy + 1)
    start_halo(0, -1)

    inputs[1].wait()
    inputs[2].wait()
    tables = []
    for m in range(eps_ref.shape[0]):
        eps = jnp.full((8, cols), eps_ref[m], F32)
        ratio = jnp.full((8, cols), sig_ref[m], F32) * TIME_STEP / (2.0 * eps)
        tables.append(((1.0 - ratio) / (1.0 + ratio), TIME_STEP / eps / (1.0 + ratio)))

    def spread(z, _):
        kind = mat_ref[z].reshape(rows // 8, 8, cols)
        dec = jnp.broadcast_to(tables[0][0][None], kind.shape)
        gai = jnp.broadcast_to(tables[0][1][None], kind.shape)
        for m in range(1, len(tables)):
            hit = kind == m
            dec = jnp.where(hit, tables[m][0][None], dec)
            gai = jnp.where(hit, tables[m][1][None], gai)
        decay[z] = dec.reshape(rows, cols)
        gain[z] = gai.reshape(rows, cols)
        return 0

    lax.fori_loop(0, nz, spread, 0)
    finish_halo(0, -1)

    for z in range(nz):
        ex, ey, ez = e_ref[0, z], e_ref[1, z], e_ref[2, z]
        if z + 1 < nz:
            dz_x, dz_y = e_ref[0, z + 1] - ex, e_ref[1, z + 1] - ey
        else:
            dz_x, dz_y = -ex, -ey
        edge = xrecv[0]

        def ahead_x(comp, j):
            far = jnp.where(
                lane == cols - 1, pltpu.roll(edge, (cols - 1 - j) % cols, 1), pltpu.roll(comp, cols - 1, 1)
            )
            return far - comp

        def ahead_y(comp, j):
            halo = jnp.broadcast_to(yrecv[0, j : j + 1, :], (rows, cols))
            return jnp.where(row == rows - 1, halo, pltpu.roll(comp, rows - 1, 0)) - comp

        curl = (
            ahead_y(ez, nz + z) - dz_y,
            dz_x - ahead_x(ez, nz + z),
            ahead_x(ey, z) - ahead_y(ex, z),
        )
        for c in range(3):
            h_out[c, z] = h_ref[c, z] - TIME_STEP * curl[c]

    pack_edges(1, h_out, cols - 1, rows - 1)
    start_halo(1, 1)
    start_wires(0, h_out)
    finish_halo(1, 1)
    start_edges()
    strip_copy.wait()
    filter_lines(0)
    filter_edges()
    back(0)
    merge(0, h_out)
    results[0].start()
    edges_back()

    kept = jnp.zeros((rows, cols), jnp.int32)
    for z in range(nz):
        kept = jnp.where(lane % nz == z, is_wire[z], kept)
    left = jnp.where(kept == 1, edge_filt[...], xrecv[1])

    for z in range(nz):
        hx, hy, hz = h_out[0, z], h_out[1, z], h_out[2, z]
        if z > 0:
            dz_x, dz_y = hx - h_out[0, z - 1], hy - h_out[1, z - 1]
        else:
            dz_x, dz_y = hx, hy
        def behind_x(comp, j):
            far = jnp.where(lane == 0, pltpu.roll(left, (cols - j) % cols, 1), pltpu.roll(comp, 1, 1))
            return comp - far

        def behind_y(comp, j):
            plane = (j // nz) * 2 * n_wires + rank[z]
            raw = jnp.broadcast_to(yrecv[1, j : j + 1, :], (rows, cols))
            filtered = jnp.broadcast_to(tails[plane][7:8], (rows, cols))
            halo = jnp.where(jnp.full((rows, cols), is_wire[z], jnp.int32) == 1, filtered, raw)
            return comp - jnp.where(row == 0, halo, pltpu.roll(comp, 1, 0))

        curl = (
            behind_y(hz, nz + z) - dz_y,
            dz_x - behind_x(hz, nz + z),
            behind_x(hy, z) - behind_y(hx, z),
        )
        for c in range(3):
            e_out[c, z] = decay[z] * e_ref[c, z] + gain[z] * curl[c]

    start_wires(1, e_out)
    filter_lines(1)
    back(1)
    merge(1, e_out)
    results[1].start()
    drain(0)
    edges_gone()
    drain(1)

    for copy in results:
        copy.wait()


def body(n_gx, n_gy, e_field, h_field, material, permittivity, conductivity, wire_layers):
    _, nz, rows, cols = e_field.shape
    n_lines = n_gy * rows
    n_wires = nz // 2
    n_planes = 3 * n_wires
    strip = jnp.asarray(filter_strip(n_lines, TILE))
    smem = pl.BlockSpec(memory_space=pltpu.SMEM)
    hbm = pl.BlockSpec(memory_space=pl.ANY)
    block = jax.ShapeDtypeStruct(e_field.shape, F32)
    dma = pltpu.SemaphoreType.DMA
    return pl.pallas_call(
        functools.partial(kernel, n_gx, n_gy, n_wires),
        out_shape=(block, block),
        in_specs=[smem, smem, smem, hbm, hbm, hbm, hbm],
        out_specs=(hbm, hbm),
        scratch_shapes=[
            pltpu.VMEM(e_field.shape, F32),
            pltpu.VMEM(h_field.shape, F32),
            pltpu.VMEM(material.shape, jnp.int32),
            pltpu.VMEM(e_field.shape, F32),
            pltpu.VMEM(h_field.shape, F32),
            pltpu.VMEM(strip.shape, BF16),
            pltpu.VMEM((2, rows, cols), F32),
            pltpu.VMEM((2, rows, cols), F32),
            pltpu.VMEM((2, 2 * nz, cols), F32),
            pltpu.VMEM((2, 2 * nz, cols), F32),
            pltpu.VMEM((2, n_planes, rows, cols), BF16),
            pltpu.VMEM((2, n_gy, rows, cols), BF16),
            pltpu.VMEM((2, n_gy, rows, cols), F32),
            pltpu.VMEM((2, n_planes, rows, cols), F32),
            pltpu.VMEM((nz, rows, cols), F32),
            pltpu.VMEM((nz, rows, cols), F32),
            pltpu.VMEM((rows, cols), BF16),
            pltpu.VMEM((n_gy, rows, cols), BF16),
            pltpu.VMEM((n_gy // 4, rows, cols), F32),
            pltpu.VMEM((rows, cols), F32),
            pltpu.VMEM((n_planes, 8, cols), F32),
            dma((2, 2)),
            dma((2, 2)),
            dma((2, n_gy // 2)),
            dma((2, n_gy)),
            dma((2, n_gy)),
            dma((2, n_planes)),
            dma,
            dma((3,)),
            dma((2,)),
            dma((4,)),
            dma((n_gy,)),
            dma((n_gy // 4,)),
            dma,
            dma((n_gy,)),
            dma((n_planes,)),
        ],
        compiler_params=pltpu.CompilerParams(collective_id=0, has_side_effects=True),
    )(permittivity, conductivity, wire_layers, e_field, h_field, material, strip)


def solution(mesh):
    field = P(None, None, "gy", "gx")
    placed = (field, field, P(None, "gy", "gx"), P(), P(), P())
    return jax.shard_map(
        functools.partial(body, mesh.shape["gx"], mesh.shape["gy"]),
        mesh=mesh,
        in_specs=placed,
        out_specs=(field, field),
        check_vma=False,
    )
```

```python
import functools
import math

import jax
import jax.numpy as jnp
import ml_dtypes
import numpy as np
from jax import lax
from jax.experimental import pallas as pl
from jax.experimental.pallas import tpu as pltpu
from jax.sharding import PartitionSpec as P

TIME_STEP = 0.9
MESH = pl.DeviceIdType.MESH
F32 = jnp.float32
BF16 = jnp.bfloat16
TILE = 256


def filter_strip(n_cols, tile):
    row_pos = np.arange(tile, dtype=np.int64)[:, None]
    col_pos = np.arange(2 * n_cols - tile, dtype=np.int64)[None, :]
    delta = row_pos - col_pos + (n_cols - tile)
    modes = 2 * (n_cols // 4) + 1
    turned = np.mod(modes * delta, 2 * n_cols)
    safe_delta = np.where(delta == 0, 1, delta)
    pi = np.float32(math.pi)
    upper = np.sin(pi * turned.astype(np.float32) / np.float32(n_cols))
    lower = np.float32(n_cols) * np.sin(pi * safe_delta.astype(np.float32) / np.float32(n_cols))
    band = np.where(delta == 0, np.float32(modes / n_cols), upper / lower)
    out = np.float32(0.7) * band + np.where(delta == 0, np.float32(0.3), np.float32(0.0))
    return out.astype(np.float32).astype(ml_dtypes.bfloat16)


def owner_on(chip):
    return chip * 2 + (chip + chip // 4) % 2


def plane_of(chip):
    return chip // 4 * 3 + (chip % 4 + 2) % 3


def edge_owner(level):
    return (level * 5) * 2 + 1


def giver_of(plane, gy):
    far = gy // 4 % 2
    spot = plane % 3
    z = jnp.where(spot == 2, 3 * far, spot + 1)
    return owner_on(plane // 3 * 4 + z)


def kernel(
    n_gx, n_gy, n_wires,
    eps_ref, sig_ref, wire_ref, e_hbm, h_hbm, mat_hbm, strip_hbm,
    e_hbm_out, h_hbm_out,
    e_ref, h_ref, mat_ref, e_out, h_out, strip, xsend, xrecv, ysend, yrecv, wires, lines, res, filt, decay, gain,
    edge_low, edge_lines, edge_res, edge_filt, tails,
    halo_send, halo_recv, wire_send, line_recv, res_send, ret_recv, strip_sem, in_sem, out_sem,
    edge_send, edge_recv, edge_give, edge_back, tail_send, tail_recv,
):
    _, nz, rows, cols = e_ref.shape
    n_planes = 3 * n_wires
    n_lines = n_gy * rows
    blocks = n_lines // TILE
    per_block = TILE // rows
    gx = lax.axis_index("gx")
    gy = lax.axis_index("gy")

    n_chips = n_gy // 2
    inputs = [
        pltpu.make_async_copy(src, dst, in_sem.at[i])
        for i, (src, dst) in enumerate(((e_hbm, e_ref), (h_hbm, h_ref), (mat_hbm, mat_ref)))
    ]
    for copy in inputs:
        copy.start()

    barrier = pltpu.get_barrier_semaphore()
    for step in (1, n_gx - 1):
        pl.semaphore_signal(
            barrier, inc=1, device_id={"gx": lax.rem(gx + step, n_gx)}, device_id_type=MESH
        )

    def greet(k, _):
        pl.semaphore_signal(
            barrier, inc=1, device_id={"gy": lax.rem(gy + k, n_gy)}, device_id_type=MESH
        )
        return 0

    lax.fori_loop(1, n_gy, greet, 0)

    strip_copy = pltpu.make_async_copy(strip_hbm, strip, strip_sem)
    strip_copy.start()

    lane = lax.broadcasted_iota(jnp.int32, (rows, cols), 1)
    row = lax.broadcasted_iota(jnp.int32, (rows, cols), 0)

    is_wire = [wire_ref[z] for z in range(nz)]
    rank, layer_of, seen = [], [jnp.int32(0)] * n_wires, jnp.int32(0)
    for z in range(nz):
        rank.append(jnp.minimum(seen, n_wires - 1))
        for k in range(n_wires):
            layer_of[k] = layer_of[k] + jnp.where((is_wire[z] == 1) & (seen == k), z, 0)
        seen = seen + is_wire[z]

    def pack_edges(phase, src, col, edge_row):
        total = jnp.zeros((rows, cols), F32)
        for c in (1, 2):
            for z in range(nz):
                j = (c - 1) * nz + z
                moved = pltpu.roll(src[c, z], (j - col) % cols, 1)
                total = jnp.where(lane == j, moved, total)
        xsend[phase] = total
        for i, c in enumerate((0, 2)):
            for z in range(nz):
                ysend[phase, i * nz + z : i * nz + z + 1, :] = src[c, z, edge_row : edge_row + 1, :]

    def halo_copies(phase, step):
        x_copy = pltpu.make_async_remote_copy(
            src_ref=xsend.at[phase],
            dst_ref=xrecv.at[phase],
            send_sem=halo_send.at[phase, 0],
            recv_sem=halo_recv.at[phase, 0],
            device_id={"gx": lax.rem(gx + step + n_gx, n_gx)},
            device_id_type=MESH,
        )
        y_copy = pltpu.make_async_remote_copy(
            src_ref=ysend.at[phase],
            dst_ref=yrecv.at[phase],
            send_sem=halo_send.at[phase, 1],
            recv_sem=halo_recv.at[phase, 1],
            device_id={"gy": lax.rem(gy + step + n_gy, n_gy)},
            device_id_type=MESH,
        )
        return x_copy, y_copy

    def start_halo(phase, step):
        x_copy, y_copy = halo_copies(phase, step)
        x_copy.start()
        sender = gy > 0 if step < 0 else gy < n_gy - 1

        @pl.when(sender)
        def _():
            y_copy.start()

    def finish_halo(phase, step):
        x_copy, y_copy = halo_copies(phase, step)
        x_copy.wait()
        sender = gy > 0 if step < 0 else gy < n_gy - 1
        receiver = gy < n_gy - 1 if step < 0 else gy > 0

        @pl.when(sender)
        def _():
            y_copy.wait_send()

        @pl.when(receiver)
        def _():
            y_copy.wait_recv()

    def start_wires(phase, src):
        for c in range(3):
            for k in range(n_wires):
                wires[phase, c * n_wires + k] = src[c, layer_of[k]].astype(BF16)

        def send(t, _):
            to = lax.rem(t + 4 + gy // 2, n_chips)
            plane = plane_of(to)
            owner = owner_on(to)

            @pl.when(owner != gy)
            def _():
                pltpu.make_async_remote_copy(
                    src_ref=wires.at[phase, plane],
                    dst_ref=lines.at[phase, gy],
                    send_sem=wire_send.at[phase, to],
                    recv_sem=line_recv.at[phase, gy],
                    device_id={"gy": owner},
                    device_id_type=MESH,
                ).start()

            @pl.when(owner == gy)
            def _():
                pltpu.make_async_copy(
                    wires.at[phase, plane], lines.at[phase, gy], line_recv.at[phase, gy]
                ).start()

            return 0

        lax.fori_loop(0, n_chips, send, 0)

    chip = gy // 2
    my_plane = plane_of(chip)
    i_own = owner_on(chip) == gy
    depth = chip % 4

    def serves(at):
        return (depth == 1) | (depth == 2) | (depth // 2 == at % 2)

    def tail_copy(plane, to):
        return pltpu.make_async_remote_copy(
            src_ref=res.at[0, to, pl.ds(rows - 8, 8)],
            dst_ref=tails.at[plane],
            send_sem=tail_send.at[to],
            recv_sem=tail_recv.at[plane],
            device_id={"gy": lax.rem(to + 1, n_gy)},
            device_id_type=MESH,
        )

    def own_tail(plane, to):
        return pltpu.make_async_copy(
            res.at[0, to, pl.ds(rows - 8, 8)], tails.at[plane], tail_recv.at[plane]
        )

    has_tails = my_plane // n_wires != 1

    def start_tail(to):
        @pl.when(has_tails & (to + 1 < n_gy) & (to + 1 != gy))
        def _():
            tail_copy(my_plane, to).start()

        @pl.when(has_tails & (to + 1 == gy))
        def _():
            own_tail(my_plane, to).start()

    level = chip % 4
    i_edge = edge_owner(level) == gy

    def edge_copy(to_level, source):
        return pltpu.make_async_remote_copy(
            src_ref=edge_low,
            dst_ref=edge_lines.at[source],
            send_sem=edge_send.at[to_level],
            recv_sem=edge_recv.at[source],
            device_id={"gy": edge_owner(to_level)},
            device_id_type=MESH,
        )

    def own_edge():
        return pltpu.make_async_copy(edge_low, edge_lines.at[gy], edge_recv.at[gy])

    def start_edges():
        edge_low[...] = xrecv[1].astype(BF16)

        def send(t, _):
            to_level = lax.rem(t + level, 4)

            @pl.when(edge_owner(to_level) != gy)
            def _():
                edge_copy(to_level, gy).start()

            @pl.when(edge_owner(to_level) == gy)
            def _():
                own_edge().start()

            return 0

        lax.fori_loop(0, 4, send, 0)

    def edge_give_copy(slot):
        return pltpu.make_async_remote_copy(
            src_ref=edge_res.at[slot],
            dst_ref=edge_filt,
            send_sem=edge_give.at[slot],
            recv_sem=edge_back,
            device_id={"gy": (slot // 2 * 4 + level) * 2 + slot % 2},
            device_id_type=MESH,
        )

    def own_edge_give(slot):
        return pltpu.make_async_copy(edge_res.at[slot], edge_filt, edge_back)

    own_slot = chip // 4 * 2 + gy % 2

    def filter_edges():
        @pl.when(i_edge)
        def _():
            def arrive(s, _):
                @pl.when(s != gy)
                def _():
                    edge_copy(level, s).wait_recv()

                @pl.when(s == gy)
                def _():
                    own_edge().wait()

                return 0

            lax.fori_loop(0, n_gy, arrive, 0)

            def block(t, _):
                run = lax.rem(t + level + 1, n_chips // 4)
                at = run * 2 + level // 2
                start = pl.multiple_of((blocks - 1 - at) * TILE, TILE)
                top = pl.multiple_of(level % 2 * (TILE // 2), TILE // 2)
                out = jnp.dot(
                    strip[pl.ds(top, TILE // 2), pl.ds(start, n_lines)],
                    edge_lines[...].reshape(n_lines, cols),
                    preferred_element_type=F32,
                )
                edge_res[pl.ds(run * 2, 2)] = out.reshape(2, rows, cols)

                def give(i, _):
                    slot = run * 2 + i

                    @pl.when(slot != own_slot)
                    def _():
                        edge_give_copy(slot).start()

                    @pl.when(slot == own_slot)
                    def _():
                        own_edge_give(slot).start()

                    return 0

                lax.fori_loop(0, 2, give, 0)
                return 0

            lax.fori_loop(0, n_chips // 4, block, 0)

    def edges_back():
        @pl.when(i_edge)
        def _():
            own_edge_give(own_slot).wait()

        @pl.when(jnp.logical_not(i_edge))
        def _():
            edge_give_copy(own_slot).wait_recv()

        @pl.when(gy > 0)
        def _():
            def arrive(t, _):
                plane = t + t // n_wires * n_wires
                giver = giver_of(plane, gy - 1)

                @pl.when(giver != gy)
                def _():
                    tail_copy(plane, gy).wait_recv()

                @pl.when(giver == gy)
                def _():
                    own_tail(plane, gy - 1).wait()

                return 0

            lax.fori_loop(0, 2 * n_wires, arrive, 0)

    def edges_gone():
        def sent(to_level, _):
            @pl.when(edge_owner(to_level) != gy)
            def _():
                edge_copy(to_level, gy).wait_send()

            return 0

        lax.fori_loop(0, 4, sent, 0)

        @pl.when(i_edge)
        def _():
            def given(slot, _):
                @pl.when(slot != own_slot)
                def _():
                    edge_give_copy(slot).wait_send()

                return 0

            lax.fori_loop(0, n_chips // 2, given, 0)

        @pl.when(i_own & has_tails)
        def _():
            def tail_gone(to, _):
                @pl.when((to + 1 != gy) & serves(to // per_block))
                def _():
                    tail_copy(my_plane, to).wait_send()

                return 0

            lax.fori_loop(0, n_gy - 1, tail_gone, 0)

    def filter_lines(phase):
        @pl.when(i_own)
        def _():
            def arrive(s, _):
                @pl.when(s != gy)
                def _():
                    pltpu.make_async_remote_copy(
                        src_ref=wires.at[phase, my_plane],
                        dst_ref=lines.at[phase, s],
                        send_sem=wire_send.at[phase, 0],
                        recv_sem=line_recv.at[phase, s],
                        device_id={"gy": s},
                        device_id_type=MESH,
                    ).wait_recv()

                @pl.when(s == gy)
                def _():
                    pltpu.make_async_copy(
                        wires.at[phase, my_plane], lines.at[phase, s], line_recv.at[phase, s]
                    ).wait()

                return 0

            lax.fori_loop(0, n_gy, arrive, 0)
            def block(t, _):
                at = lax.rem(t + chip // 2, blocks)

                @pl.when(serves(at))
                def _():
                    start = pl.multiple_of((blocks - 1 - at) * TILE, TILE)
                    out = jnp.dot(
                        strip[:, pl.ds(start, n_lines)],
                        lines[phase].reshape(n_lines, cols),
                        preferred_element_type=F32,
                    )
                    res[phase, pl.ds(at * per_block, per_block)] = out.reshape(per_block, rows, cols)

                    def give(i, _):
                        to = at * per_block + i

                        @pl.when(to != gy)
                        def _():
                            pltpu.make_async_remote_copy(
                                src_ref=res.at[phase, to],
                                dst_ref=filt.at[phase, my_plane],
                                send_sem=res_send.at[phase, to],
                                recv_sem=ret_recv.at[phase, my_plane],
                                device_id={"gy": to},
                                device_id_type=MESH,
                            ).start()

                        @pl.when(to == gy)
                        def _():
                            pltpu.make_async_copy(
                                res.at[phase, to], filt.at[phase, my_plane], ret_recv.at[phase, my_plane]
                            ).start()

                        if phase == 0:
                            start_tail(to)
                        return 0

                    lax.fori_loop(0, per_block, give, 0)
                return 0


            lax.fori_loop(0, blocks, block, 0)

    def back(phase):
        def arrive(plane, _):
            owner = giver_of(plane, gy)

            @pl.when(owner != gy)
            def _():
                pltpu.make_async_remote_copy(
                    src_ref=res.at[phase, gy],
                    dst_ref=filt.at[phase, plane],
                    send_sem=res_send.at[phase, gy],
                    recv_sem=ret_recv.at[phase, plane],
                    device_id={"gy": owner},
                    device_id_type=MESH,
                ).wait_recv()

            @pl.when(owner == gy)
            def _():
                pltpu.make_async_copy(
                    res.at[phase, gy], filt.at[phase, plane], ret_recv.at[phase, plane]
                ).wait()

            return 0

        lax.fori_loop(0, n_planes, arrive, 0)

    def drain(phase):
        def wire_gone(to, _):
            owner = owner_on(to)

            @pl.when(owner != gy)
            def _():
                pltpu.make_async_remote_copy(
                    src_ref=wires.at[phase, plane_of(to)],
                    dst_ref=lines.at[phase, gy],
                    send_sem=wire_send.at[phase, to],
                    recv_sem=line_recv.at[phase, gy],
                    device_id={"gy": owner},
                    device_id_type=MESH,
                ).wait_send()

            return 0

        lax.fori_loop(0, n_chips, wire_gone, 0)

        @pl.when(i_own)
        def _():
            def row_gone(to, _):
                @pl.when((to != gy) & serves(to // per_block))
                def _():
                    pltpu.make_async_remote_copy(
                        src_ref=res.at[phase, to],
                        dst_ref=filt.at[phase, my_plane],
                        send_sem=res_send.at[phase, to],
                        recv_sem=ret_recv.at[phase, my_plane],
                        device_id={"gy": to},
                        device_id_type=MESH,
                    ).wait_send()

                return 0

            lax.fori_loop(0, n_gy, row_gone, 0)

    def merge(phase, dst):
        for z in range(nz):
            chosen = jnp.full((rows, cols), is_wire[z], jnp.int32) == 1
            for c in range(3):
                dst[c, z] = jnp.where(chosen, filt[phase, c * n_wires + rank[z]], dst[c, z])
            if phase == 1:
                results[z].start()

    results = [
        pltpu.make_async_copy(e_out.at[:, z], e_hbm_out.at[:, z], out_sem.at[z]) for z in range(nz)
    ]
    results.append(pltpu.make_async_copy(h_out, h_hbm_out, out_sem.at[nz]))

    inputs[0].wait()
    pack_edges(0, e_ref, 0, 0)

    @pl.when(gy == n_gy - 1)
    def _():
        yrecv[0] = jnp.zeros((2 * nz, cols), F32)

    @pl.when(gy == 0)
    def _():
        yrecv[1] = jnp.zeros((2 * nz, cols), F32)
        tails[...] = jnp.zeros(tails.shape, F32)

    pl.semaphore_wait(barrier, n_gy + 1)
    start_halo(0, -1)

    inputs[1].wait()
    inputs[2].wait()
    tables = []
    for m in range(eps_ref.shape[0]):
        eps = jnp.full((8, cols), eps_ref[m], F32)
        ratio = jnp.full((8, cols), sig_ref[m], F32) * TIME_STEP / (2.0 * eps)
        tables.append(((1.0 - ratio) / (1.0 + ratio), TIME_STEP / eps / (1.0 + ratio)))

    def spread(z, _):
        kind = mat_ref[z].reshape(rows // 8, 8, cols)
        dec = jnp.broadcast_to(tables[0][0][None], kind.shape)
        gai = jnp.broadcast_to(tables[0][1][None], kind.shape)
        for m in range(1, len(tables)):
            hit = kind == m
            dec = jnp.where(hit, tables[m][0][None], dec)
            gai = jnp.where(hit, tables[m][1][None], gai)
        decay[z] = dec.reshape(rows, cols)
        gain[z] = gai.reshape(rows, cols)
        return 0

    lax.fori_loop(0, nz, spread, 0)
    finish_halo(0, -1)

    for z in range(nz):
        ex, ey, ez = e_ref[0, z], e_ref[1, z], e_ref[2, z]
        if z + 1 < nz:
            dz_x, dz_y = e_ref[0, z + 1] - ex, e_ref[1, z + 1] - ey
        else:
            dz_x, dz_y = -ex, -ey
        edge = xrecv[0]

        def ahead_x(comp, j):
            far = jnp.where(
                lane == cols - 1, pltpu.roll(edge, (cols - 1 - j) % cols, 1), pltpu.roll(comp, cols - 1, 1)
            )
            return far - comp

        def ahead_y(comp, j):
            halo = jnp.broadcast_to(yrecv[0, j : j + 1, :], (rows, cols))
            return jnp.where(row == rows - 1, halo, pltpu.roll(comp, rows - 1, 0)) - comp

        curl = (
            ahead_y(ez, nz + z) - dz_y,
            dz_x - ahead_x(ez, nz + z),
            ahead_x(ey, z) - ahead_y(ex, z),
        )
        for c in range(3):
            h_out[c, z] = h_ref[c, z] - TIME_STEP * curl[c]

    pack_edges(1, h_out, cols - 1, rows - 1)
    start_halo(1, 1)
    start_wires(0, h_out)
    finish_halo(1, 1)
    start_edges()
    strip_copy.wait()
    filter_lines(0)
    filter_edges()
    back(0)
    merge(0, h_out)
    results[nz].start()
    edges_back()

    kept = jnp.zeros((rows, cols), jnp.int32)
    for z in range(nz):
        kept = jnp.where(lane % nz == z, is_wire[z], kept)
    left = jnp.where(kept == 1, edge_filt[...], xrecv[1])

    for z in range(nz):
        hx, hy, hz = h_out[0, z], h_out[1, z], h_out[2, z]
        if z > 0:
            dz_x, dz_y = hx - h_out[0, z - 1], hy - h_out[1, z - 1]
        else:
            dz_x, dz_y = hx, hy
        def behind_x(comp, j):
            far = jnp.where(lane == 0, pltpu.roll(left, (cols - j) % cols, 1), pltpu.roll(comp, 1, 1))
            return comp - far

        def behind_y(comp, j):
            plane = (j // nz) * 2 * n_wires + rank[z]
            raw = jnp.broadcast_to(yrecv[1, j : j + 1, :], (rows, cols))
            filtered = jnp.broadcast_to(tails[plane][7:8], (rows, cols))
            halo = jnp.where(jnp.full((rows, cols), is_wire[z], jnp.int32) == 1, filtered, raw)
            return comp - jnp.where(row == 0, halo, pltpu.roll(comp, 1, 0))

        curl = (
            behind_y(hz, nz + z) - dz_y,
            dz_x - behind_x(hz, nz + z),
            behind_x(hy, z) - behind_y(hx, z),
        )
        for c in range(3):
            e_out[c, z] = decay[z] * e_ref[c, z] + gain[z] * curl[c]

    start_wires(1, e_out)
    filter_lines(1)
    back(1)
    merge(1, e_out)
    drain(0)
    edges_gone()
    drain(1)

    for copy in results:
        copy.wait()


def body(n_gx, n_gy, e_field, h_field, material, permittivity, conductivity, wire_layers):
    _, nz, rows, cols = e_field.shape
    n_lines = n_gy * rows
    n_wires = nz // 2
    n_planes = 3 * n_wires
    strip = jnp.asarray(filter_strip(n_lines, TILE))
    smem = pl.BlockSpec(memory_space=pltpu.SMEM)
    hbm = pl.BlockSpec(memory_space=pl.ANY)
    block = jax.ShapeDtypeStruct(e_field.shape, F32)
    dma = pltpu.SemaphoreType.DMA
    return pl.pallas_call(
        functools.partial(kernel, n_gx, n_gy, n_wires),
        out_shape=(block, block),
        in_specs=[smem, smem, smem, hbm, hbm, hbm, hbm],
        out_specs=(hbm, hbm),
        scratch_shapes=[
            pltpu.VMEM(e_field.shape, F32),
            pltpu.VMEM(h_field.shape, F32),
            pltpu.VMEM(material.shape, jnp.int32),
            pltpu.VMEM(e_field.shape, F32),
            pltpu.VMEM(h_field.shape, F32),
            pltpu.VMEM(strip.shape, BF16),
            pltpu.VMEM((2, rows, cols), F32),
            pltpu.VMEM((2, rows, cols), F32),
            pltpu.VMEM((2, 2 * nz, cols), F32),
            pltpu.VMEM((2, 2 * nz, cols), F32),
            pltpu.VMEM((2, n_planes, rows, cols), BF16),
            pltpu.VMEM((2, n_gy, rows, cols), BF16),
            pltpu.VMEM((2, n_gy, rows, cols), F32),
            pltpu.VMEM((2, n_planes, rows, cols), F32),
            pltpu.VMEM((nz, rows, cols), F32),
            pltpu.VMEM((nz, rows, cols), F32),
            pltpu.VMEM((rows, cols), BF16),
            pltpu.VMEM((n_gy, rows, cols), BF16),
            pltpu.VMEM((n_gy // 4, rows, cols), F32),
            pltpu.VMEM((rows, cols), F32),
            pltpu.VMEM((n_planes, 8, cols), F32),
            dma((2, 2)),
            dma((2, 2)),
            dma((2, n_gy // 2)),
            dma((2, n_gy)),
            dma((2, n_gy)),
            dma((2, n_planes)),
            dma,
            dma((3,)),
            dma((nz + 1,)),
            dma((4,)),
            dma((n_gy,)),
            dma((n_gy // 4,)),
            dma,
            dma((n_gy,)),
            dma((n_planes,)),
        ],
        compiler_params=pltpu.CompilerParams(collective_id=0, has_side_effects=True),
    )(permittivity, conductivity, wire_layers, e_field, h_field, material, strip)


def solution(mesh):
    field = P(None, None, "gy", "gx")
    placed = (field, field, P(None, "gy", "gx"), P(), P(), P())
    return jax.shard_map(
        functools.partial(body, mesh.shape["gx"], mesh.shape["gy"]),
        mesh=mesh,
        in_specs=placed,
        out_specs=(field, field),
        check_vma=False,
    )
```
